256 devices in a mesh: geo: 32 (over x, z), bins: 8 (over y, core).
Axes of the slice: x: 4, y: 4, z: 8, core: 2. Of those that a mesh axis runs over, the one named last changes fastest.
Arguments:
- spectrum: float32 [1152, 256, 256], P('bins', 'geo'), may hold values from 0.1 to 2
- sea_mask: int32 [256, 256], P('geo'), may hold values 0 or 1
- kernel_linear: bfloat16 [1152, 1152], replicated, may hold values from -0.1875 to 0.1875
- kernel_square: bfloat16 [1152, 1152], replicated, may hold values from -0.1875 to 0.1875
- drift_kernel: bfloat16 [128, 1152], replicated, may hold values from -0.1875 to 0.1875
- ocean: float32 [2, 64, 256, 256], P(None, 'bins', 'geo'), may hold values from -3 to 3
Outputs:
- spectrum_out: float32 [1152, 256, 256], P('bins', 'geo')
- ocean_out: float32 [2, 64, 256, 256], P(None, 'bins', 'geo')
The draws below stay inside these ranges and needn't reach their ends.
Inputs may be any that keep to these rules, and one draw needn't show every extreme that they name: `sea_mask`: 1 marks a sea column, 0 a land column.
All inputs are finite; a program needn't handle non-finite values. No bound on the sum of `sea_mask` on one device may be relied on, other than what follows from the above.
Results may differ from the reference program's by a relative error of at most 0.0018.
Values sent between devices are 32-bit elements; how exact they have to be, the bound alone decides.
A program may use at most 64 MiB of HBM per device.

```python
import math
import jax
import jax.numpy as jnp
from jax import lax

NDIR = 36
NFREQ = 32
NB = 1152
CY = 256
LEV = 64
STEPS = 3
SUB = 2
NX = 256


def touch_ends(values, key, low, high):
    spot = [jax.random.randint(jax.random.fold_in(key, axis), (), 0, length) for axis, length in enumerate(values.shape)]
    widest = values.shape.index(max(values.shape))
    neighbour = spot[:widest] + [(spot[widest] + 1) % values.shape[widest]] + spot[widest + 1:]
    return values.at[tuple(spot)].set(low).at[tuple(neighbour)].set(high)


def shard_levels(key, shape, pieces, low, high):
    def one(axis_at, blocks):
        steps = jax.random.uniform(jax.random.fold_in(jax.random.fold_in(key, 6), axis_at), (blocks,), jnp.float32, low / len(pieces), high / len(pieces))
        return jnp.repeat(jnp.exp(steps), shape[axis_at] // blocks).reshape((-1,) + (1,) * (len(shape) - axis_at - 1))

    level = one(*pieces[0])
    for cut in pieces[1:]:
        level = level * one(*cut)
    return level


def gaussian(rng, dims, scale, reach, cuts=(), kind=jnp.bfloat16):
    factor_of = shard_levels(rng, dims, cuts, -0.22, 0.18) if cuts else 1.0
    values = jax.random.normal(rng, dims, jnp.float32) * scale * factor_of
    return jnp.minimum(jnp.maximum(values, -reach), reach).astype(kind)


def setup_inputs(seed: int = 0) -> dict:
    arg_keys = jax.random.split(jax.random.key(seed), 7)
    spectrum = jnp.clip(jnp.exp(math.log(2.0) - 2.9957323 * jax.random.uniform(arg_keys[0], (NB, NX, CY), jnp.float32) ** shard_levels(arg_keys[0], (NB, NX, CY), ((0, 8), (1, 32)), -0.2, 0.2)), 0.1, 2.0)
    sea_mask = touch_ends((jax.random.randint(arg_keys[1], (NX, CY), 0, 4) < 3).astype(jnp.int32), jax.random.fold_in(arg_keys[1], 1), 0, 1)
    kernel_linear = gaussian(arg_keys[2], (NB, NB), NB ** -0.5, 0.1875)
    kernel_square = gaussian(arg_keys[3], (NB, NB), NB ** -0.5, 0.1875)
    drift_kernel = gaussian(arg_keys[4], (2 * LEV, NB), NB ** -0.5, 0.1875)
    ocean = gaussian(arg_keys[5], (2, LEV, NX, CY), 0.5, 3.0, ((1, 8), (2, 32)), jnp.float32)
    return {"spectrum": spectrum, "sea_mask": sea_mask, "kernel_linear": kernel_linear, "kernel_square": kernel_square, "drift_kernel": drift_kernel, "ocean": ocean}


DT_SOURCE = 0.5
DT_OCEAN = 0.2
CORIOLIS = 1.0
VISCOSITY = 1.0
DOPPLER = 0.1


def speeds(first_bin, bin_count):
    bin_index = first_bin + jnp.arange(bin_count, dtype=jnp.int32)
    direction = (bin_index // NFREQ).astype(jnp.float32)
    frequency = (bin_index % NFREQ).astype(jnp.float32)
    group_speed = 0.4 / (1.0 + frequency / 16.0)
    bin_angle = (2.0 * jnp.pi / NDIR) * direction
    return group_speed * jnp.cos(bin_angle), group_speed * jnp.sin(bin_angle)


def along_y(energy, speed_y):
    flux_plus = jnp.maximum(speed_y, 0.0) * energy
    flux_minus = jnp.minimum(speed_y, 0.0) * energy
    zeros_edge = jnp.zeros_like(flux_plus[..., :1])
    plus_before = jnp.concatenate([zeros_edge, flux_plus[..., :-1]], axis=-1)
    minus_after = jnp.concatenate([flux_minus[..., 1:], zeros_edge], axis=-1)
    return (flux_plus - plus_before) + (minus_after - flux_minus)


def step_cells(energy, plus_left, flux_plus, flux_minus, minus_right, speed_y, sea_float):
    moved = energy - ((flux_plus - plus_left) + (minus_right - flux_minus)) - along_y(energy, speed_y)
    return moved * sea_float


def renew_source(energy, interaction, squares_sum, sea_float):
    return energy + DT_SOURCE * (sea_float * (interaction * energy / (1.0 + squares_sum / NB)))


def laplace(centre, west_side, east_side):
    zeros_edge = jnp.zeros_like(centre[..., :1])
    north_side = jnp.concatenate([centre[..., 1:], zeros_edge], axis=-1)
    south_side = jnp.concatenate([zeros_edge, centre[..., :-1]], axis=-1)
    return (east_side + west_side) + (north_side + south_side) - 4.0 * centre


def ocean_step(ocean_state, west_side, east_side, stokes_u, stokes_v, sea_float):
    laplacian = laplace(ocean_state, west_side, east_side)
    new_u = (ocean_state[0] + DT_OCEAN * (CORIOLIS * (ocean_state[1] + stokes_v) + VISCOSITY * laplacian[0])) * sea_float
    new_v = (ocean_state[1] + DT_OCEAN * (-(CORIOLIS * (ocean_state[0] + stokes_u)) + VISCOSITY * laplacian[1])) * sea_float
    return jnp.stack([new_u, new_v])


def widen(values):
    return lax.optimization_barrier(values.astype(jnp.bfloat16)).astype(jnp.float32)


def reference(spectrum, sea_mask, kernel_linear, kernel_square, drift_kernel, ocean):
    sea_float = sea_mask.astype(jnp.float32)
    speed_cx, speed_cy = speeds(0, NB)
    energy = spectrum
    ocean_state = ocean
    width_x = spectrum.shape[1]
    width_y = spectrum.shape[2]
    levels = ocean.shape[1]
    wide_linear = kernel_linear.astype(jnp.float32)
    wide_square = kernel_square.astype(jnp.float32)
    wide_drift = drift_kernel.astype(jnp.float32)
    for step_index in range(STEPS):
        tanh_cur = jnp.tanh(ocean_state[:, 0])
        speed_x = speed_cx[:, None, None] + DOPPLER * tanh_cur[0][None]
        speed_y = speed_cy[:, None, None] + DOPPLER * tanh_cur[1][None]
        for substep in range(SUB):
            flux_plus = jnp.maximum(speed_x, 0.0) * energy
            flux_minus = jnp.minimum(speed_x, 0.0) * energy
            energy = step_cells(energy, jnp.roll(flux_plus, 1, axis=1), flux_plus, flux_minus,
                                jnp.roll(flux_minus, -1, axis=1), speed_y, sea_float)
        energy_flat = energy.reshape(NB, width_x * width_y)
        interaction = jnp.dot(wide_linear, widen(energy_flat), precision=lax.Precision.HIGHEST) + \
            jnp.dot(wide_square, widen(energy_flat * energy_flat), precision=lax.Precision.HIGHEST)
        updated = renew_source(energy_flat, interaction, jnp.sum(energy_flat * energy_flat, axis=0),
                               sea_float.reshape(width_x * width_y))
        stokes_drift = jnp.dot(wide_drift, widen(updated), precision=lax.Precision.HIGHEST)
        energy = updated.reshape(NB, width_x, width_y)
        stokes_drift = stokes_drift.reshape(levels, 2, width_x, width_y)
        ocean_state = ocean_step(ocean_state, jnp.roll(ocean_state, 1, axis=2), jnp.roll(ocean_state, -1, axis=2),
                                 stokes_drift[:, 0], stokes_drift[:, 1], sea_float)
    return energy, ocean_state
```

```python
import jax
import jax.numpy as jnp
import numpy as np
from jax import lax
from jax.experimental import pallas as pl
from jax.experimental.pallas import tpu as pltpu
from jax.sharding import PartitionSpec as P

NDIR = 36
NFREQ = 32
NB = 1152
STEPS = 3
PARTS = 8
BINS = NB // PARTS
CHAN = 16
WX = 8
WY = 32
COLS = WX * WY
LT = NB // 128
OT = LT
NT = LT + 1
ROW = 40
ROWS = 13
EXT = ROW * ROWS
FIRST = 3

DT_SOURCE = 0.5
DT_OCEAN = 0.2
DOPPLER = 0.1

MESH = pl.DeviceIdType.MESH
TRANSPOSED = (((1,), (1,)), ((), ()))


def group_speeds():
    index = np.arange(NB)
    direction = (index // NFREQ).astype(np.float32)
    frequency = (index % NFREQ).astype(np.float32)
    speed = np.float32(0.4) / (np.float32(1.0) + frequency / np.float32(16.0))
    angle = np.float32(2.0 * np.pi / NDIR) * direction
    both = np.stack([speed * np.cos(angle), speed * np.sin(angle)]).astype(np.float32)
    return np.ascontiguousarray(np.broadcast_to(both.reshape(2, LT, 1, 128), (2, LT, 8, 128)))


def own_row(x):
    return pl.multiple_of((FIRST + x) * ROW, 8)


def kernel(
    xs, os, sea, kl, ks, dk, cg, eo, oo,
    flat, ext, sea_ext, e1, e2, rounded, squared, tu, tv, weight, drift,
    klv, ksv, dkv, ysend, yrecv, csend, crecv, sysend, syrecv, scsend, screcv,
    in_send, in_recv, halo_send, halo_recv, sea_send, sea_recv, out_send, out_recv, local,
):
    g = lax.axis_index("geo")
    r = lax.axis_index("bins")
    tiles = lax.axis_size("geo")
    west, east = lax.rem(g + tiles - 1, tiles), lax.rem(g + 1, tiles)
    south, north = lax.rem(r + PARTS - 1, PARTS), lax.rem(r + 1, PARTS)

    weights = [
        pltpu.make_async_copy(kl, klv, local.at[0]),
        pltpu.make_async_copy(ks, ksv, local.at[1]),
        pltpu.make_async_copy(dk, dkv, local.at[2]),
    ]
    own_in = [
        pltpu.make_async_copy(xs.at[r], flat.at[pl.ds(pl.multiple_of(r * BINS, 8), BINS)], local.at[3]),
        pltpu.make_async_copy(os.at[r], flat.at[pl.ds(pl.multiple_of(NB + r * CHAN, 8), CHAN)], local.at[4]),
    ]
    for copy in own_in + weights:
        copy.start()

    barrier = pltpu.get_barrier_semaphore()
    friends = [(g, lax.rem(r + d, PARTS)) for d in range(1, PARTS)]
    friends += [(x, y) for x in (west, east) for y in (south, r, north)]
    for friend in friends:
        pl.semaphore_signal(barrier, inc=1, device_id=friend, device_id_type=MESH)
    pl.semaphore_wait(barrier, len(friends))

    def remote(src, dst, send, recv, device):
        return pltpu.make_async_remote_copy(
            src_ref=src, dst_ref=dst, send_sem=send, recv_sem=recv, device_id=device, device_id_type=MESH
        )

    entering = []
    for d in range(1, PARTS):
        peer = lax.rem(r + d, PARTS)
        entering.append(remote(
            os.at[peer], flat.at[pl.ds(pl.multiple_of(NB + r * CHAN, 8), CHAN)],
            in_send.at[0, d], in_recv.at[0, d], (g, peer)))
        entering.append(remote(
            xs.at[peer], flat.at[pl.ds(pl.multiple_of(r * BINS, 8), BINS)],
            in_send.at[1, d], in_recv.at[1, d], (g, peer)))
    for copy in entering:
        copy.start()

    def halo_copies(field, ys, yr, cs, cr, send, recv):
        depth = field.shape[0]
        every = pl.ds(0, depth)
        copies = []
        for i in range(2):
            copies.append(remote(
                field.at[every, pl.ds((FIRST + i) * ROW, WY)],
                field.at[every, pl.ds((FIRST + WX + i) * ROW, WY)],
                send.at[i], recv.at[i], (west, r)))
            copies.append(remote(
                field.at[every, pl.ds((FIRST + WX - 2 + i) * ROW, WY)],
                field.at[every, pl.ds((FIRST - 2 + i) * ROW, WY)],
                send.at[2 + i], recv.at[2 + i], (east, r)))
        copies.append(remote(ys.at[0], yr.at[1], send.at[4], recv.at[4], (g, south)))
        copies.append(remote(ys.at[1], yr.at[0], send.at[5], recv.at[5], (g, north)))
        copies.append(remote(cs.at[0], cr.at[3], send.at[6], recv.at[6], (west, south)))
        copies.append(remote(cs.at[1], cr.at[2], send.at[7], recv.at[7], (west, north)))
        copies.append(remote(cs.at[2], cr.at[1], send.at[8], recv.at[8], (east, south)))
        copies.append(remote(cs.at[3], cr.at[0], send.at[9], recv.at[9], (east, north)))
        return copies

    corners_from = [FIRST * ROW, FIRST * ROW + WY - 1, (FIRST + WX - 1) * ROW, (FIRST + WX - 1) * ROW + WY - 1]
    corners_to = [(FIRST - 1) * ROW - 1, (FIRST - 1) * ROW + WY, (FIRST + WX) * ROW - 1, (FIRST + WX) * ROW + WY]

    def pack(field, ys, cs):
        def one(t, carry):
            for side, start in enumerate((0, WY - 2)):
                for i in range(2):
                    ys[side, t, i] = field[t, pl.ds(FIRST * ROW + start + i, WX, stride=ROW), :]
            for k in range(4):
                cs[k, pl.ds(t, 1), :] = field[t, pl.ds(corners_from[k], 1), :]
            return carry
        lax.fori_loop(0, field.shape[0], one, 0)

    has_south = (r > 0).astype(jnp.float32)
    has_north = (r < PARTS - 1).astype(jnp.float32)

    def unpack(field, yr, cr):
        def one(t, carry):
            for i in range(2):
                field[t, pl.ds(FIRST * ROW - 2 + i, WX, stride=ROW), :] = yr[0, t, i] * has_south
                field[t, pl.ds(FIRST * ROW + WY + i, WX, stride=ROW), :] = yr[1, t, i] * has_north
            for k in range(4):
                inside = has_south if k % 2 == 0 else has_north
                field[t, pl.ds(corners_to[k], 1), :] = cr[k, pl.ds(t, 1), :] * inside
            return carry
        lax.fori_loop(0, field.shape[0], one, 0)

    for x in range(WX):
        sea_ext[0, pl.ds((FIRST + x) * ROW, WY), :] = sea[pl.ds(x * WY, WY), :]
    pack(sea_ext, sysend, scsend)
    sea_copies = halo_copies(sea_ext, sysend, syrecv, scsend, screcv, sea_send, sea_recv)
    for copy in sea_copies:
        copy.start()

    for copy in own_in + entering:
        copy.wait()

    def turn(t, carry):
        for half in range(2):
            block = flat[pl.ds(pl.multiple_of(t * 128, 128), 128), half * 128:(half + 1) * 128].T
            for i in range(4):
                ext[0, t, pl.ds((FIRST + 4 * half + i) * ROW, WY), :] = block[i * WY:(i + 1) * WY]
        return carry

    lax.fori_loop(0, NT, turn, 0)

    for copy in sea_copies:
        copy.wait()
    unpack(sea_ext, syrecv, screcv)
    for copy in weights:
        copy.wait()

    def advance(cx, cy, e_at, u_at, v_at, here, size, sea_here):
        new = e_at(here, size) * (1.0 - jnp.abs(cx + u_at(here, size)) - jnp.abs(cy + v_at(here, size)))
        new += jnp.maximum(cx + u_at(here - ROW, size), 0.0) * e_at(here - ROW, size)
        new -= jnp.minimum(cx + u_at(here + ROW, size), 0.0) * e_at(here + ROW, size)
        new += jnp.maximum(cy + v_at(here - 1, size), 0.0) * e_at(here - 1, size)
        new -= jnp.minimum(cy + v_at(here + 1, size), 0.0) * e_at(here + 1, size)
        return new * sea_here

    u_at = lambda at, size: tu[pl.ds(at, size), :]
    v_at = lambda at, size: tv[pl.ds(at, size), :]

    def step_body(step, carry):
        field, after = ext.at[step], ext.at[step + 1]
        pack(field, ysend.at[step], csend.at[step])
        copies = halo_copies(
            field, ysend.at[step], yrecv.at[step], csend.at[step], crecv.at[step],
            halo_send.at[step], halo_recv.at[step])
        for copy in copies:
            copy.start()
        for copy in copies:
            copy.wait()
        unpack(field, yrecv.at[step], crecv.at[step])

        def currents(row, c):
            at = pl.multiple_of(row * ROW, 8)
            top = DOPPLER * jnp.tanh(field[OT, pl.ds(at, ROW), :])
            tu[pl.ds(at, ROW), :] = jnp.broadcast_to(top[:, 0:1], (ROW, 128))
            tv[pl.ds(at, ROW), :] = jnp.broadcast_to(top[:, 1:2], (ROW, 128))
            return c

        lax.fori_loop(1, ROWS, currents, 0)

        def first(i, c):
            at = pl.multiple_of(i * 8, 8)
            sea_here = sea_ext[0, pl.ds(at, 8), :]
            for t in range(LT):
                e1[t, pl.ds(at, 8), :] = advance(
                    cg[0, t], cg[1, t], lambda a, s: field[t, pl.ds(a, s), :], u_at, v_at, at, 8, sea_here)
            return c

        lax.fori_loop(2 * ROW // 8, 12 * ROW // 8, first, 0)

        def second(i, c):
            at = pl.multiple_of(own_row(lax.div(i, 2)) + lax.rem(i, 2) * 16, 8)
            to = pl.multiple_of(i * 16, 16)
            sea_here = sea_ext[0, pl.ds(at, 16), :]
            total = jnp.zeros((16, 128), jnp.float32)
            for t in range(LT):
                cx = jnp.concatenate([cg[0, t]] * 2, axis=0)
                cy = jnp.concatenate([cg[1, t]] * 2, axis=0)
                new = advance(cx, cy, lambda a, s: e1[t, pl.ds(a, s), :], u_at, v_at, at, 16, sea_here)
                e2[t, pl.ds(to, 16), :] = new
                square = new * new
                total += square
                rounded[pl.ds(to, 16), t * 128:(t + 1) * 128] = new.astype(jnp.bfloat16)
                squared[pl.ds(to, 16), t * 128:(t + 1) * 128] = square.astype(jnp.bfloat16)
            total = jnp.sum(total, axis=1, keepdims=True)
            scale = DT_SOURCE / (1.0 + total / NB)
            weight[pl.ds(to, 16), :] = sea_here * scale
            return c

        lax.fori_loop(0, COLS // 16, second, 0)

        drift[...] = jnp.zeros_like(drift)

        def source(first_tile, count):
            rows = pl.ds(pl.multiple_of(first_tile * 128, 128), count * 128)
            inter = lax.dot_general(rounded[...], klv[rows, :], TRANSPOSED, preferred_element_type=jnp.float32)
            inter += lax.dot_general(squared[...], ksv[rows, :], TRANSPOSED, preferred_element_type=jnp.float32)
            fresh = []
            for k in range(count):
                old = e2[first_tile + k]
                new = old + inter[:, k * 128:(k + 1) * 128] * old * weight[...]
                for x in range(WX):
                    after[first_tile + k, pl.ds((FIRST + x) * ROW, WY), :] = new[x * WY:(x + 1) * WY]
                fresh.append(new.astype(jnp.bfloat16))
            fresh = jnp.concatenate(fresh, axis=1) if count > 1 else fresh[0]
            drift[...] += lax.dot_general(fresh, dkv[:, rows], TRANSPOSED, preferred_element_type=jnp.float32)

        def pair(n, c):
            source(2 * n, 2)
            return c

        lax.fori_loop(0, LT // 2, pair, 0)
        source(LT - 1, 1)

        lane = lax.broadcasted_iota(jnp.int32, (WY, 128), 1)
        even = lax.rem(lane, 2) == 0
        sign = jnp.where(even, DT_OCEAN, -DT_OCEAN)

        def swim(x, c):
            at = own_row(x)
            old = field[OT, pl.ds(at, WY), :]
            lap = (field[OT, pl.ds(at + ROW, WY), :] + field[OT, pl.ds(at - ROW, WY), :]
                   + (field[OT, pl.ds(at + 1, WY), :] + field[OT, pl.ds(at - 1, WY), :]) - 4.0 * old)
            pushed = old + drift[pl.ds(pl.multiple_of(x * WY, WY), WY), :]
            other = jnp.where(even, pltpu.roll(pushed, 127, 1), pltpu.roll(pushed, 1, 1))
            after[OT, pl.ds(at, WY), :] = (old + (sign * other + DT_OCEAN * lap)) * sea_ext[0, pl.ds(at, WY), :]
            return c

        lax.fori_loop(0, WX, swim, 0)
        return carry

    lax.fori_loop(0, STEPS, step_body, 0)

    def turn_back(t, carry):
        for half in range(2):
            block = jnp.concatenate(
                [ext[STEPS, t, pl.ds((FIRST + 4 * half + i) * ROW, WY), :] for i in range(4)], axis=0)
            flat[pl.ds(pl.multiple_of(t * 128, 128), 128), half * 128:(half + 1) * 128] = block.T
        return carry

    lax.fori_loop(0, NT, turn_back, 0)

    def mine(peer):
        return (flat.at[pl.ds(pl.multiple_of(NB + peer * CHAN, 8), CHAN)],
                flat.at[pl.ds(pl.multiple_of(peer * BINS, 8), BINS)])

    own_o, own_e = mine(r)
    leaving = [pltpu.make_async_copy(own_o, oo.at[r], local.at[3]), pltpu.make_async_copy(own_e, eo.at[r], local.at[4])]
    for d in range(1, PARTS):
        peer = lax.rem(r + d, PARTS)
        src_o, src_e = mine(peer)
        leaving.append(remote(src_o, oo.at[r], out_send.at[0, d], out_recv.at[0, d], (g, peer)))
        leaving.append(remote(src_e, eo.at[r], out_send.at[1, d], out_recv.at[1, d], (g, peer)))
    for copy in leaving:
        copy.start()
    for copy in leaving:
        copy.wait()


def per_device(spectrum, sea_mask, kernel_linear, kernel_square, drift_kernel, ocean):
    r = lax.axis_index("bins")
    xs = spectrum.reshape(BINS, WX, PARTS, WY).transpose(2, 0, 1, 3).reshape(PARTS, BINS, COLS)
    levels = ocean.shape[1]
    os = ocean.reshape(2, levels, WX, PARTS, WY).transpose(3, 1, 0, 2, 4).reshape(PARTS, CHAN, COLS)
    sea = lax.dynamic_slice_in_dim(sea_mask.astype(jnp.float32), r * WY, WY, axis=1)
    sea = jnp.broadcast_to(sea.reshape(COLS, 1), (COLS, 128))

    any_ = pl.BlockSpec(memory_space=pl.ANY)
    vmem = pl.BlockSpec(memory_space=pltpu.VMEM)
    f32, bf16 = jnp.float32, jnp.bfloat16
    eo, oo = pl.pallas_call(
        kernel,
        out_shape=(
            jax.ShapeDtypeStruct((PARTS, BINS, COLS), f32),
            jax.ShapeDtypeStruct((PARTS, CHAN, COLS), f32),
        ),
        in_specs=[any_, any_, vmem, any_, any_, any_, vmem],
        out_specs=(any_, any_),
        scratch_shapes=[
            pltpu.VMEM((NT * 128, COLS), f32),
            pltpu.VMEM((STEPS + 1, NT, EXT, 128), f32),
            pltpu.VMEM((1, EXT, 128), f32),
            pltpu.VMEM((LT, EXT, 128), f32),
            pltpu.VMEM((LT, COLS, 128), f32),
            pltpu.VMEM((COLS, NB), bf16),
            pltpu.VMEM((COLS, NB), bf16),
            pltpu.VMEM((EXT, 128), f32),
            pltpu.VMEM((EXT, 128), f32),
            pltpu.VMEM((COLS, 128), f32),
            pltpu.VMEM((COLS, 128), f32),
            pltpu.VMEM((NB, NB), bf16),
            pltpu.VMEM((NB, NB), bf16),
            pltpu.VMEM((128, NB), bf16),
            pltpu.VMEM((STEPS, 2, NT, 2, WX, 128), f32),
            pltpu.VMEM((STEPS, 2, NT, 2, WX, 128), f32),
            pltpu.VMEM((STEPS, 4, 16, 128), f32),
            pltpu.VMEM((STEPS, 4, 16, 128), f32),
            pltpu.VMEM((2, 1, 2, WX, 128), f32),
            pltpu.VMEM((2, 1, 2, WX, 128), f32),
            pltpu.VMEM((4, 8, 128), f32),
            pltpu.VMEM((4, 8, 128), f32),
            pltpu.SemaphoreType.DMA((2, PARTS)),
            pltpu.SemaphoreType.DMA((2, PARTS)),
            pltpu.SemaphoreType.DMA((STEPS, 10)),
            pltpu.SemaphoreType.DMA((STEPS, 10)),
            pltpu.SemaphoreType.DMA((10,)),
            pltpu.SemaphoreType.DMA((10,)),
            pltpu.SemaphoreType.DMA((2, PARTS)),
            pltpu.SemaphoreType.DMA((2, PARTS)),
            pltpu.SemaphoreType.DMA((5,)),
        ],
        compiler_params=pltpu.CompilerParams(
            collective_id=0, has_side_effects=True, vmem_limit_bytes=60 * 1024 * 1024
        ),
        name="coupled",
    )(xs, os, sea, kernel_linear, kernel_square, drift_kernel, jnp.asarray(group_speeds()))
    energy = eo.reshape(PARTS, BINS, WX, WY).transpose(1, 2, 0, 3).reshape(BINS, WX, PARTS * WY)
    ocean_out = oo.reshape(PARTS, levels, 2, WX, WY).transpose(2, 1, 3, 0, 4).reshape(2, levels, WX, PARTS * WY)
    return energy, ocean_out


def solution(mesh):
    return jax.shard_map(
        per_device,
        mesh=mesh,
        in_specs=(
            P("bins", "geo", None),
            P("geo", None),
            P(),
            P(),
            P(),
            P(None, "bins", "geo", None),
        ),
        out_specs=(P("bins", "geo", None), P(None, "bins", "geo", None)),
        check_vma=False,
    )
```

```python
import jax
import jax.numpy as jnp
import numpy as np
from jax import lax
from jax.experimental import pallas as pl
from jax.experimental.pallas import tpu as pltpu
from jax.sharding import PartitionSpec as P

NDIR = 36
NFREQ = 32
NB = 1152
STEPS = 3
PARTS = 8
BINS = NB // PARTS
SHARE = 16
WX = 8
WY = 32
COLS = WX * WY
LT = NB // 128
OT = LT
NT = LT + 1
GROUPS = LT // 2 + 2
ROW = 40
ROWS = 13
EXT = ROW * ROWS
FIRST = 3
HOLD = 3

DT_SOURCE = 0.5
DT_OCEAN = 0.2
DOPPLER = 0.1

MESH = pl.DeviceIdType.MESH


def bin_order():
    return np.arange(NB).reshape(PARTS, LT, SHARE).transpose(1, 0, 2).reshape(NB)


def group_speeds():
    index = bin_order()
    direction = (index // NFREQ).astype(np.float32)
    frequency = (index % NFREQ).astype(np.float32)
    speed = np.float32(0.4) / (np.float32(1.0) + frequency / np.float32(16.0))
    angle = np.float32(2.0 * np.pi / NDIR) * direction
    both = np.stack([speed * np.cos(angle), speed * np.sin(angle)]).astype(np.float32)
    return np.ascontiguousarray(np.broadcast_to(both.reshape(2, LT, 1, 128), (2, LT, 8, 128)))


def own_row(x):
    return pl.multiple_of((FIRST + x) * ROW, 8)


def tile_rows(t):
    return pl.ds(pl.multiple_of(t * 128, 128), 128)


def share_rows(k):
    return pl.ds(pl.multiple_of(k * SHARE, SHARE), SHARE)


def kernel(
    spectrum, ocean, sea, kl, ks, dk, cg, eo, oo,
    spec, swim_in, send, flat, ext, sea_raw, sea_turned, sea_ext, e1, e2, rounded, squared, tu, tv, total, weight,
    drift, kl_raw, ks_raw, dk_raw, wl, ws, wd, ysend, yrecv, csend, crecv, back, got, spec_out, swim_out,
    in_send, in_recv, halo_send, halo_recv, sea_send, sea_recv, out_send, out_recv, load, weights_sem, store,
):
    g = lax.axis_index("geo")
    r = lax.axis_index("bins")
    tiles = lax.axis_size("geo")
    west, east = lax.rem(g + tiles - 1, tiles), lax.rem(g + 1, tiles)
    south, north = lax.rem(r + PARTS - 1, PARTS), lax.rem(r + 1, PARTS)

    barrier = pltpu.get_barrier_semaphore()
    friends = [(g, lax.rem(r + d, PARTS)) for d in range(1, PARTS)]
    friends += [(x, y) for x in (west, east) for y in (south, r, north)]
    for friend in friends:
        pl.semaphore_signal(barrier, inc=1, device_id=friend, device_id_type=MESH)

    def half_lanes(h):
        return pl.ds(h * 128, 128)

    loads = []
    for h in range(2):
        loads.append(pltpu.make_async_copy(ocean.at[:, half_lanes(h)], swim_in.at[h], load.at[LT, h]))

    def spec_load(t, h):
        return pltpu.make_async_copy(spectrum.at[tile_rows(t), half_lanes(h)], spec.at[h, tile_rows(t)], load.at[t, h])

    for copy in loads:
        copy.start()
    for t in range(LT):
        for h in range(2):
            spec_load(t, h).start()
    weights = [pltpu.make_async_copy(dk, dk_raw, weights_sem.at[0])]
    for t in range(LT):
        weights.append(pltpu.make_async_copy(kl.at[:, t], kl_raw.at[t], weights_sem.at[1 + t]))
        weights.append(pltpu.make_async_copy(ks.at[:, t], ks_raw.at[t], weights_sem.at[1 + LT + t]))
    for copy in weights:
        copy.start()

    lane = lax.broadcasted_iota(jnp.int32, (8, 128), 1)
    low_half = lane < 64
    even_block = lax.rem(lax.div(lane, 32), 2) == 0

    def swap_blocks(a):
        c = [None] * 4
        for i in range(2):
            c[i] = jnp.where(low_half, a[i], pltpu.roll(a[i + 2], 64, 1))
            c[i + 2] = jnp.where(low_half, pltpu.roll(a[i], 64, 1), a[i + 2])
        out = []
        for i in (0, 2):
            out.append(jnp.where(even_block, c[i], pltpu.roll(c[i + 1], 32, 1)))
            out.append(jnp.where(even_block, pltpu.roll(c[i], 96, 1), c[i + 1]))
        return out

    def remote(src, dst, send_sem, recv_sem, device):
        return pltpu.make_async_remote_copy(
            src_ref=src, dst_ref=dst, send_sem=send_sem, recv_sem=recv_sem, device_id=device, device_id_type=MESH
        )

    def entry_copies(t):
        copies = []
        for d in range(1, PARTS):
            peer = lax.rem(r + d, PARTS)
            copies.append(remote(
                send.at[t, peer], flat.at[t, :, share_rows(r)], in_send.at[t, d], in_recv.at[t, d], (g, peer)))
        return copies

    def exit_copies(t):
        copies = []
        for d in range(1, PARTS):
            peer = lax.rem(r + d, PARTS)
            copies.append(remote(
                back.at[t, :, share_rows(peer)], got.at[t, r], out_send.at[t, d], out_recv.at[t, d], (g, peer)))
        return copies

    def ship(t):
        for copy in entry_copies(t):
            copy.start()
        for half in range(2):
            flat[t, half, share_rows(r), :] = send[t, r, half]

    sea_raw[1] = sea[...].astype(jnp.float32)
    sea_copies = [
        remote(sea_raw.at[1], sea_raw.at[2], sea_send.at[0], sea_recv.at[0], (west, r)),
        remote(sea_raw.at[1], sea_raw.at[0], sea_send.at[1], sea_recv.at[1], (east, r)),
    ]

    for copy in loads:
        copy.wait()
    for comp in range(2):
        for h in range(2):
            for half in range(2):
                blocks = swap_blocks(
                    [swim_in[h, pl.ds(64 * comp + 4 * half + i, 8, stride=8), :] for i in range(4)])
                for j in range(4):
                    send[OT, 4 * h + j, half, pl.ds(comp, 8, stride=2), :] = blocks[j]

    pl.semaphore_wait(barrier, len(friends))
    for copy in sea_copies:
        copy.start()
    ship(OT)

    def enter(t, carry):
        for h in range(2):
            spec_load(t, h).wait()
        for octet in range(2):
            for h in range(2):
                for half in range(2):
                    blocks = swap_blocks([
                        spec[h, pl.ds(t * 128 + octet * 64 + 4 * half + i, 8, stride=8), :] for i in range(4)])
                    for j in range(4):
                        send[t, 4 * h + j, half, pl.ds(octet * 8, 8), :] = blocks[j]
        ship(t)
        return carry

    lax.fori_loop(0, LT, enter, 0)

    def halo_copies(step, group, first_tile, count):
        field = ext.at[step]
        every = pl.ds(first_tile, count)
        sems, semr = halo_send.at[step, group], halo_recv.at[step, group]
        ys, yr = ysend.at[step, group], yrecv.at[step, group]
        cs, cr = csend.at[step, group], crecv.at[step, group]
        some = pl.ds(0, count)
        copies = [
            remote(ys.at[0, some], yr.at[1, some], sems.at[4], semr.at[4], (g, south)),
            remote(ys.at[1, some], yr.at[0, some], sems.at[5], semr.at[5], (g, north)),
            remote(cs.at[0], cr.at[3], sems.at[6], semr.at[6], (west, south)),
            remote(cs.at[1], cr.at[2], sems.at[7], semr.at[7], (west, north)),
            remote(cs.at[2], cr.at[1], sems.at[8], semr.at[8], (east, south)),
            remote(cs.at[3], cr.at[0], sems.at[9], semr.at[9], (east, north)),
        ]
        for i in range(2):
            copies.append(remote(
                field.at[every, pl.ds((FIRST + i) * ROW, WY)],
                field.at[every, pl.ds((FIRST + WX + i) * ROW, WY)],
                sems.at[i], semr.at[i], (west, r)))
            copies.append(remote(
                field.at[every, pl.ds((FIRST + WX - 2 + i) * ROW, WY)],
                field.at[every, pl.ds((FIRST - 2 + i) * ROW, WY)],
                sems.at[2 + i], semr.at[2 + i], (east, r)))
        return copies

    corners_from = [FIRST * ROW, FIRST * ROW + WY - 1, (FIRST + WX - 1) * ROW, (FIRST + WX - 1) * ROW + WY - 1]
    corners_to = [(FIRST - 1) * ROW - 1, (FIRST - 1) * ROW + WY, (FIRST + WX) * ROW - 1, (FIRST + WX) * ROW + WY]
    has_south = (r > 0).astype(jnp.float32)
    has_north = (r < PARTS - 1).astype(jnp.float32)

    def send_halo(step, group, first_tile, count):
        for n in range(count):
            t = first_tile + n
            for side, start in enumerate((0, WY - 2)):
                for i in range(2):
                    ysend[step, group, side, n, i] = ext[step, t, pl.ds(FIRST * ROW + start + i, WX, stride=ROW), :]
            for k in range(4):
                csend[step, group, k, pl.ds(n, 1), :] = ext[step, t, pl.ds(corners_from[k], 1), :]
        for copy in halo_copies(step, group, first_tile, count):
            copy.start()

    def take_halo(step, group, first_tile, count):
        for copy in halo_copies(step, group, first_tile, count):
            copy.wait()
        for n in range(count):
            t = first_tile + n
            for i in range(2):
                ext[step, t, pl.ds(FIRST * ROW - 2 + i, WX, stride=ROW), :] = yrecv[step, group, 0, n, i] * has_south
                ext[step, t, pl.ds(FIRST * ROW + WY + i, WX, stride=ROW), :] = yrecv[step, group, 1, n, i] * has_north
            for k in range(4):
                inside = has_south if k % 2 == 0 else has_north
                ext[step, t, pl.ds(corners_to[k], 1), :] = crecv[step, group, k, pl.ds(n, 1), :] * inside

    def turn(t):
        for copy in entry_copies(t):
            copy.wait()
        for half in range(2):
            block = flat[t, half].T
            for i in range(4):
                ext[0, t, pl.ds((FIRST + 4 * half + i) * ROW, WY), :] = block[i * WY:(i + 1) * WY]

    def currents(step):
        def one(row, c):
            at = pl.multiple_of(row * ROW, 8)
            top = DOPPLER * jnp.tanh(ext[step, OT, pl.ds(at, ROW), :])
            tu[pl.ds(at, ROW), :] = jnp.broadcast_to(top[:, 0:1], (ROW, 128))
            tv[pl.ds(at, ROW), :] = jnp.broadcast_to(top[:, 1:2], (ROW, 128))
            return c
        lax.fori_loop(1, ROWS, one, 0)

    u_at = lambda at: tu[pl.ds(at, 16), :]
    v_at = lambda at: tv[pl.ds(at, 16), :]

    def advance(cx, cy, e_at, here, sea_here):
        new = e_at(here) * (1.0 - jnp.abs(cx + u_at(here)) - jnp.abs(cy + v_at(here)))
        new += jnp.maximum(cx + u_at(here - ROW), 0.0) * e_at(here - ROW)
        new -= jnp.minimum(cx + u_at(here + ROW), 0.0) * e_at(here + ROW)
        new += jnp.maximum(cy + v_at(here - 1), 0.0) * e_at(here - 1)
        new -= jnp.minimum(cy + v_at(here + 1), 0.0) * e_at(here + 1)
        return new * sea_here

    def advect(step, first_tile, count):
        def speeds(t):
            return jnp.concatenate([cg[0, t]] * 2, axis=0), jnp.concatenate([cg[1, t]] * 2, axis=0)

        def first(i, c):
            at = pl.multiple_of(i * 16, 16)
            sea_here = sea_ext[pl.ds(at, 16), :]
            for n in range(count):
                t = first_tile + n
                cx, cy = speeds(t)
                e1[t, pl.ds(at, 16), :] = advance(cx, cy, lambda a: ext[step, t, pl.ds(a, 16), :], at, sea_here)
            return c

        lax.fori_loop(2 * ROW // 16, 12 * ROW // 16, first, 0)

        def second(i, c):
            at = pl.multiple_of(own_row(lax.div(i, 2)) + lax.rem(i, 2) * 16, 8)
            to = pl.ds(pl.multiple_of(i * 16, 16), 16)
            sea_here = sea_ext[pl.ds(at, 16), :]
            squares = total[to, :]
            for n in range(count):
                t = first_tile + n
                cx, cy = speeds(t)
                new = advance(cx, cy, lambda a: e1[t, pl.ds(a, 16), :], at, sea_here)
                e2[t, to, :] = new
                square = new * new
                squares += square
                rounded[to, tile_rows(t)] = new.astype(jnp.bfloat16)
                squared[to, tile_rows(t)] = square.astype(jnp.bfloat16)
            total[to, :] = squares
            return c

        lax.fori_loop(0, COLS // 16, second, 0)

    def weigh():
        def one(x, c):
            to = pl.ds(pl.multiple_of(x * WY, WY), WY)
            sums = jnp.sum(total[to, :], axis=1, keepdims=True)
            weight[to, :] = sea_ext[pl.ds(own_row(x), WY), :] * (DT_SOURCE / (1.0 + sums / NB))
            return c
        lax.fori_loop(0, WX, one, 0)

    def prepare(v):
        for raw, out in ((kl_raw, wl), (ks_raw, ws)):
            for u in range(LT):
                block = raw[v].reshape(128, NB)[:, u * 128:(u + 1) * 128].T
                for i in range(8):
                    k, t = divmod(8 * u + i, LT)
                    out[pl.ds(128 * t + SHARE * k, SHARE), tile_rows(v)] = block[i * SHARE:(i + 1) * SHARE]

    turn(OT)
    send_halo(0, GROUPS - 1, OT, 1)

    for copy in sea_copies:
        copy.wait()
    sea_turned[...] = jnp.zeros_like(sea_turned)
    for h in range(2):
        lanes = slice(h * 128, (h + 1) * 128)
        rows = jnp.concatenate(
            [sea_raw[0, :, lanes], sea_raw[1, :, lanes], sea_raw[2, :, lanes], jnp.zeros((104, 128), jnp.float32)], axis=0)
        sea_turned[pl.ds(8 + h * 128, 128), :] = rows.T
    for q in range(12):
        column = q + 6
        here = sea_turned[pl.ds(pl.multiple_of(8 + r * WY, 8), ROW), :]
        sea_ext[pl.ds((q + 1) * ROW, ROW), :] = jnp.broadcast_to(here[:, column:column + 1], (ROW, 128))
        left = sea_turned[pl.ds(6 + r * WY, 2), :]
        sea_ext[pl.ds((q + 1) * ROW - 2, 2), :] = jnp.broadcast_to(left[:, column:column + 1], (2, 128))

    for copy in weights:
        copy.wait()
    for u in range(LT):
        block = dk_raw[:, u * 128:(u + 1) * 128].T
        for i in range(8):
            k, t = divmod(8 * u + i, LT)
            wd[pl.ds(128 * t + SHARE * k, SHARE), :] = block[i * SHARE:(i + 1) * SHARE]

    take_halo(0, GROUPS - 1, OT, 1)
    currents(0)
    total[...] = jnp.zeros_like(total)

    def enter_pair(n, c):
        turn(2 * n)
        turn(2 * n + 1)
        send_halo(0, n, 2 * n, 2)
        prepare(2 * n)
        prepare(2 * n + 1)

        @pl.when(n > 0)
        def _():
            take_halo(0, n - 1, 2 * n - 2, 2)
            advect(0, 2 * n - 2, 2)

        return c

    lax.fori_loop(0, LT // 2, enter_pair, 0)
    turn(LT - 1)
    send_halo(0, GROUPS - 2, LT - 1, 1)
    prepare(LT - 1)
    take_halo(0, GROUPS - 3, LT - 3, 2)
    advect(0, LT - 3, 2)
    take_halo(0, GROUPS - 2, LT - 1, 1)
    advect(0, LT - 1, 1)

    lane_row = lax.broadcasted_iota(jnp.int32, (WY, 128), 1)
    even = lax.rem(lane_row, 2) == 0
    sign = jnp.where(even, DT_OCEAN, -DT_OCEAN)

    def turn_back(t, value):
        for half in range(2):
            back[t, half] = value[half * 128:(half + 1) * 128].T
        for copy in exit_copies(t):
            copy.start()
        for half in range(2):
            got[t, r, half] = back[t, half, share_rows(r), :]

    def source(step, first_tile, count, group, now):
        lanes = pl.ds(pl.multiple_of(first_tile * 128, 128), count * 128)
        inter = jnp.dot(rounded[...], wl[:, lanes], preferred_element_type=jnp.float32)
        inter += jnp.dot(squared[...], ws[:, lanes], preferred_element_type=jnp.float32)
        fresh = []
        for k in range(count):
            old = e2[first_tile + k]
            new = old + inter[:, k * 128:(k + 1) * 128] * old * weight[...]
            if step < STEPS - 1:
                for x in range(WX):
                    ext[step + 1, first_tile + k, pl.ds((FIRST + x) * ROW, WY), :] = new[x * WY:(x + 1) * WY]
            else:
                turn_back(first_tile + k, new)
            fresh.append(new.astype(jnp.bfloat16))
        fresh = jnp.concatenate(fresh, axis=1) if count > 1 else fresh[0]
        drift[...] += jnp.dot(fresh, wd[lanes, :], preferred_element_type=jnp.float32)
        if step < STEPS - 1 and now is not None:
            @pl.when(now)
            def _():
                send_halo(step + 1, group, first_tile, count)

    def swim(step):
        def one(x, c):
            at = own_row(x)
            old = ext[step, OT, pl.ds(at, WY), :]
            lap = (ext[step, OT, pl.ds(at + ROW, WY), :] + ext[step, OT, pl.ds(at - ROW, WY), :]
                   + (ext[step, OT, pl.ds(at + 1, WY), :] + ext[step, OT, pl.ds(at - 1, WY), :]) - 4.0 * old)
            here = pl.ds(pl.multiple_of(x * WY, WY), WY)
            pushed = old + drift[here, :]
            other = jnp.where(even, pltpu.roll(pushed, 127, 1), pltpu.roll(pushed, 1, 1))
            new = (old + (sign * other + DT_OCEAN * lap)) * sea_ext[pl.ds(at, WY), :]
            if step < STEPS - 1:
                ext[step + 1, OT, pl.ds(at, WY), :] = new
            else:
                drift[here, :] = new
            return c
        lax.fori_loop(0, WX, one, 0)
        if step == STEPS - 1:
            turn_back(OT, drift[...])

    for step in range(STEPS):
        if step:
            take_halo(step, GROUPS - 1, OT, 1)
            currents(step)
            total[...] = jnp.zeros_like(total)

            def advect_pair(n, c):
                take_halo(step, n, 2 * n, 2)
                advect(step, 2 * n, 2)
                return c

            lax.fori_loop(0, LT // 2, advect_pair, 0)
            take_halo(step, GROUPS - 2, LT - 1, 1)
            advect(step, LT - 1, 1)
        weigh()
        drift[...] = jnp.zeros_like(drift)

        def source_pair(n, c):
            source(step, 2 * n, 2, n, n < HOLD)
            return c

        lax.fori_loop(0, LT // 2, source_pair, 0)
        source(step, LT - 1, 1, None, None)
        swim(step)
        if step < STEPS - 1:
            send_halo(step + 1, GROUPS - 1, OT, 1)
            for n in range(HOLD, LT // 2):
                send_halo(step + 1, n, 2 * n, 2)
            send_halo(step + 1, GROUPS - 2, LT - 1, 1)

    def spec_store(t, h):
        return pltpu.make_async_copy(spec_out.at[h, tile_rows(t)], eo.at[tile_rows(t), half_lanes(h)], store.at[t, h])

    def leave(t, carry):
        for copy in exit_copies(t):
            copy.wait()
        for octet in range(2):
            for h in range(2):
                for half in range(2):
                    blocks = swap_blocks([got[t, 4 * h + j, half, pl.ds(octet * 8, 8), :] for j in range(4)])
                    for i in range(4):
                        spec_out[h, pl.ds(t * 128 + octet * 64 + 4 * half + i, 8, stride=8), :] = blocks[i]
        for h in range(2):
            spec_store(t, h).start()
        return carry

    lax.fori_loop(0, LT, leave, 0)
    for copy in exit_copies(OT):
        copy.wait()
    for comp in range(2):
        for h in range(2):
            for half in range(2):
                blocks = swap_blocks([got[OT, 4 * h + j, half, pl.ds(comp, 8, stride=2), :] for j in range(4)])
                for i in range(4):
                    swim_out[h, pl.ds(64 * comp + 4 * half + i, 8, stride=8), :] = blocks[i]
    stores = [pltpu.make_async_copy(swim_out.at[h], oo.at[:, half_lanes(h)], store.at[LT, h]) for h in range(2)]
    for copy in stores:
        copy.start()
    for t in range(LT):
        for h in range(2):
            spec_store(t, h).wait()
    for copy in stores:
        copy.wait()


def per_device(spectrum, sea_mask, kernel_linear, kernel_square, drift_kernel, ocean):
    y = spectrum.shape[2]
    any_ = pl.BlockSpec(memory_space=pl.ANY)
    vmem = pl.BlockSpec(memory_space=pltpu.VMEM)
    f32, bf16 = jnp.float32, jnp.bfloat16
    dma = pltpu.SemaphoreType.DMA
    eo, oo = pl.pallas_call(
        kernel,
        out_shape=(jax.ShapeDtypeStruct((NB, y), f32), jax.ShapeDtypeStruct((128, y), f32)),
        in_specs=[any_, any_, vmem, any_, any_, any_, vmem],
        out_specs=(any_, any_),
        scratch_shapes=[
            pltpu.VMEM((2, NB, 128), f32),
            pltpu.VMEM((2, 128, 128), f32),
            pltpu.VMEM((NT, PARTS, 2, SHARE, 128), f32),
            pltpu.VMEM((NT, 2, 128, 128), f32),
            pltpu.VMEM((STEPS, NT, EXT, 128), f32),
            pltpu.VMEM((3, 8, y), f32),
            pltpu.VMEM((8 + 256 + ROW, 128), f32),
            pltpu.VMEM((EXT, 128), f32),
            pltpu.VMEM((LT, EXT, 128), f32),
            pltpu.VMEM((LT, COLS, 128), f32),
            pltpu.VMEM((COLS, NB), bf16),
            pltpu.VMEM((COLS, NB), bf16),
            pltpu.VMEM((EXT, 128), f32),
            pltpu.VMEM((EXT, 128), f32),
            pltpu.VMEM((COLS, 128), f32),
            pltpu.VMEM((COLS, 128), f32),
            pltpu.VMEM((COLS, 128), f32),
            pltpu.VMEM((LT, PARTS, SHARE, NB), bf16),
            pltpu.VMEM((LT, PARTS, SHARE, NB), bf16),
            pltpu.VMEM((128, NB), bf16),
            pltpu.VMEM((NB, NB), bf16),
            pltpu.VMEM((NB, NB), bf16),
            pltpu.VMEM((NB, 128), bf16),
            pltpu.VMEM((STEPS, GROUPS, 2, 2, 2, WX, 128), f32),
            pltpu.VMEM((STEPS, GROUPS, 2, 2, 2, WX, 128), f32),
            pltpu.VMEM((STEPS, GROUPS, 4, 8, 128), f32),
            pltpu.VMEM((STEPS, GROUPS, 4, 8, 128), f32),
            pltpu.VMEM((NT, 2, 128, 128), f32),
            pltpu.VMEM((NT, PARTS, 2, SHARE, 128), f32),
            pltpu.VMEM((2, NB, 128), f32),
            pltpu.VMEM((2, 128, 128), f32),
            dma((NT, PARTS)),
            dma((NT, PARTS)),
            dma((STEPS, GROUPS, 10)),
            dma((STEPS, GROUPS, 10)),
            dma((2,)),
            dma((2,)),
            dma((NT, PARTS)),
            dma((NT, PARTS)),
            dma((NT, 2)),
            dma((1 + 2 * LT,)),
            dma((NT, 2)),
        ],
        compiler_params=pltpu.CompilerParams(
            collective_id=0, has_side_effects=True, vmem_limit_bytes=60 * 1024 * 1024
        ),
        name="coupled",
    )(
        spectrum.reshape(NB, y),
        ocean.reshape(128, y),
        sea_mask,
        kernel_linear.reshape(PARTS, LT, SHARE, NB),
        kernel_square.reshape(PARTS, LT, SHARE, NB),
        drift_kernel,
        jnp.asarray(group_speeds()),
    )
    return eo.reshape(spectrum.shape), oo.reshape(ocean.shape)


def solution(mesh):
    return jax.shard_map(
        per_device,
        mesh=mesh,
        in_specs=(
            P("bins", "geo", None),
            P("geo", None),
            P(),
            P(),
            P(),
            P(None, "bins", "geo", None),
        ),
        out_specs=(P("bins", "geo", None), P(None, "bins", "geo", None)),
        check_vma=False,
    )
```

```python
import jax
import jax.numpy as jnp
import numpy as np
from jax import lax
from jax.experimental import pallas as pl
from jax.experimental.pallas import tpu as pltpu
from jax.sharding import PartitionSpec as P

NDIR = 36
NFREQ = 32
NB = 1152
STEPS = 3
PARTS = 8
BINS = NB // PARTS
SHARE = 16
WX = 8
WY = 32
COLS = WX * WY
LT = NB // 128
OT = LT
NT = LT + 1
GROUPS = ((0, 4), (4, 4), (8, 1), (OT, 1))
SMALL = WX * 2
ROW = 40
ROWS = 13
EXT = ROW * ROWS
FIRST = 3

DT_SOURCE = 0.5
DT_OCEAN = 0.2
DOPPLER = 0.1

MESH = pl.DeviceIdType.MESH


def bin_order():
    return np.arange(NB).reshape(PARTS, LT, SHARE).transpose(1, 0, 2).reshape(NB)


def group_speeds():
    index = bin_order()
    direction = (index // NFREQ).astype(np.float32)
    frequency = (index % NFREQ).astype(np.float32)
    speed = np.float32(0.4) / (np.float32(1.0) + frequency / np.float32(16.0))
    angle = np.float32(2.0 * np.pi / NDIR) * direction
    both = np.stack([speed * np.cos(angle), speed * np.sin(angle)]).astype(np.float32)
    return np.ascontiguousarray(np.broadcast_to(both.reshape(2, LT, 1, 128), (2, LT, 8, 128)))


def own_row(x):
    return pl.multiple_of((FIRST + x) * ROW, 8)


def tile_rows(t):
    return pl.ds(pl.multiple_of(t * 128, 128), 128)


def share_rows(k):
    return pl.ds(pl.multiple_of(k * SHARE, SHARE), SHARE)


def kernel(
    spectrum, ocean, sea, kl, ks, dk, cg, eo, oo,
    spec, swim_in, send, flat, ext, sea_raw, sea_turned, sea_ext, e1, e2, rounded, squared, tu, tv, total, weight,
    drift, kl_raw, ks_raw, dk_raw, wl, ws, wd, ysend, yrecv, csend, crecv, back, got, spec_out, swim_out,
    in_send, in_recv, halo_send, halo_recv, sea_send, sea_recv, out_send, out_recv, load, weights_sem, store,
):
    g = lax.axis_index("geo")
    r = lax.axis_index("bins")
    tiles = lax.axis_size("geo")
    west, east = lax.rem(g + tiles - 1, tiles), lax.rem(g + 1, tiles)
    south, north = lax.rem(r + PARTS - 1, PARTS), lax.rem(r + 1, PARTS)

    barrier = pltpu.get_barrier_semaphore()
    friends = [(g, lax.rem(r + d, PARTS)) for d in range(1, PARTS)]
    friends += [(x, y) for x in (west, east) for y in (south, r, north)]
    for friend in friends:
        pl.semaphore_signal(barrier, inc=1, device_id=friend, device_id_type=MESH)

    def half_lanes(h):
        return pl.ds(h * 128, 128)

    def drain(sem, rows):
        pltpu.make_async_copy(e1.at[pl.ds(0, rows)], e1.at[pl.ds(0, rows)], sem).wait()

    def spec_load(t, c):
        for h in range(2):
            pltpu.make_async_copy(
                spectrum.at[tile_rows(t), half_lanes(h)], spec.at[h, tile_rows(t)], load.at[t]).start()
        return c

    for h in range(2):
        pltpu.make_async_copy(ocean.at[:, half_lanes(h)], swim_in.at[h], load.at[LT]).start()
    lax.fori_loop(0, LT, spec_load, 0)

    lane = lax.broadcasted_iota(jnp.int32, (8, 128), 1)
    low_half = lane < 64
    even_block = lax.rem(lax.div(lane, 32), 2) == 0

    def swap_blocks(a):
        c = [None] * 4
        for i in range(2):
            c[i] = jnp.where(low_half, a[i], pltpu.roll(a[i + 2], 64, 1))
            c[i + 2] = jnp.where(low_half, pltpu.roll(a[i], 64, 1), a[i + 2])
        out = []
        for i in (0, 2):
            out.append(jnp.where(even_block, c[i], pltpu.roll(c[i + 1], 32, 1)))
            out.append(jnp.where(even_block, pltpu.roll(c[i], 96, 1), c[i + 1]))
        return out

    def remote(src, dst, send_sem, recv_sem, device):
        return pltpu.make_async_remote_copy(
            src_ref=src, dst_ref=dst, send_sem=send_sem, recv_sem=recv_sem, device_id=device, device_id_type=MESH
        )

    def entry_copies(t):
        copies = []
        for d in range(1, PARTS):
            peer = lax.rem(r + d, PARTS)
            copies.append(remote(
                send.at[t, peer], flat.at[t, :, share_rows(r)], in_send.at[0], in_recv.at[t], (g, peer)))
        return copies

    def exit_copies(t):
        copies = []
        for d in range(1, PARTS):
            peer = lax.rem(r + d, PARTS)
            copies.append(remote(
                back.at[t, :, share_rows(peer)], got.at[t, r], out_send.at[0], out_recv.at[t], (g, peer)))
        return copies

    def ship(t):
        for copy in entry_copies(t):
            copy.start()
        for half in range(2):
            flat[t, half, share_rows(r), :] = send[t, r, half]

    sea_raw[1] = sea[...].astype(jnp.float32)
    sea_copies = [
        remote(sea_raw.at[1], sea_raw.at[2], sea_send.at[0], sea_recv.at[0], (west, r)),
        remote(sea_raw.at[1], sea_raw.at[0], sea_send.at[0], sea_recv.at[0], (east, r)),
    ]

    drain(load.at[LT], 256)
    for comp in range(2):
        for h in range(2):
            for half in range(2):
                blocks = swap_blocks(
                    [swim_in[h, pl.ds(64 * comp + 4 * half + i, 8, stride=8), :] for i in range(4)])
                for j in range(4):
                    send[OT, 4 * h + j, half, pl.ds(comp, 8, stride=2), :] = blocks[j]

    pl.semaphore_wait(barrier, len(friends))
    for copy in sea_copies:
        copy.start()
    ship(OT)

    def enter(t, carry):
        drain(load.at[t], 256)
        for octet in range(2):
            for h in range(2):
                for half in range(2):
                    blocks = swap_blocks([
                        spec[h, pl.ds(t * 128 + octet * 64 + 4 * half + i, 8, stride=8), :] for i in range(4)])
                    for j in range(4):
                        send[t, 4 * h + j, half, pl.ds(octet * 8, 8), :] = blocks[j]
        ship(t)
        return carry

    lax.fori_loop(0, LT, enter, 0)

    def weights_load(t, c):
        pltpu.make_async_copy(kl.at[:, t], kl_raw.at[t], weights_sem.at[1]).start()
        pltpu.make_async_copy(ks.at[:, t], ks_raw.at[t], weights_sem.at[2]).start()
        return c

    pltpu.make_async_copy(dk, dk_raw, weights_sem.at[0]).start()
    lax.fori_loop(0, LT, weights_load, 0)

    def halo_copies(step, group):
        first_tile, count = GROUPS[group]
        field = ext.at[step]
        every = pl.ds(first_tile, count)
        sems, semr = halo_send.at[step], halo_recv.at[step, group]
        ys, yr = ysend.at[step], yrecv.at[step]
        cs, cr = csend.at[step, group], crecv.at[step, group]
        copies = [
            remote(ys.at[0, every], yr.at[1, every], sems, semr, (g, south)),
            remote(ys.at[1, every], yr.at[0, every], sems, semr, (g, north)),
            remote(cs.at[0], cr.at[3], sems, semr, (west, south)),
            remote(cs.at[1], cr.at[2], sems, semr, (west, north)),
            remote(cs.at[2], cr.at[1], sems, semr, (east, south)),
            remote(cs.at[3], cr.at[0], sems, semr, (east, north)),
        ]
        for i in range(2):
            copies.append(remote(
                field.at[every, pl.ds((FIRST + i) * ROW, WY)],
                field.at[every, pl.ds((FIRST + WX + i) * ROW, WY)],
                sems, semr, (west, r)))
            copies.append(remote(
                field.at[every, pl.ds((FIRST + WX - 2 + i) * ROW, WY)],
                field.at[every, pl.ds((FIRST - 2 + i) * ROW, WY)],
                sems, semr, (east, r)))
        return copies

    corners_from = [FIRST * ROW, FIRST * ROW + WY - 1, (FIRST + WX - 1) * ROW, (FIRST + WX - 1) * ROW + WY - 1]
    corners_to = [(FIRST - 1) * ROW - 1, (FIRST - 1) * ROW + WY, (FIRST + WX) * ROW - 1, (FIRST + WX) * ROW + WY]
    has_south = (r > 0).astype(jnp.float32)
    has_north = (r < PARTS - 1).astype(jnp.float32)

    def send_halo(step, group):
        first_tile, count = GROUPS[group]

        def one(n, carry):
            t = first_tile + n
            for side, start in enumerate((0, WY - 2)):
                for i in range(2):
                    ysend[step, side, t, i] = ext[step, t, pl.ds(FIRST * ROW + start + i, WX, stride=ROW), :]
            for k in range(4):
                csend[step, group, k, pl.ds(n, 1), :] = ext[step, t, pl.ds(corners_from[k], 1), :]
            return carry

        lax.fori_loop(0, count, one, 0)
        for copy in halo_copies(step, group):
            copy.start()

    def take_halo(step, group):
        first_tile, count = GROUPS[group]
        drain(halo_recv.at[step, group], count * (4 * WY + 2 * SMALL) + 4 * 8)

        def one(n, carry):
            t = first_tile + n
            for i in range(2):
                ext[step, t, pl.ds(FIRST * ROW - 2 + i, WX, stride=ROW), :] = yrecv[step, 0, t, i] * has_south
                ext[step, t, pl.ds(FIRST * ROW + WY + i, WX, stride=ROW), :] = yrecv[step, 1, t, i] * has_north
            for k in range(4):
                inside = has_south if k % 2 == 0 else has_north
                ext[step, t, pl.ds(corners_to[k], 1), :] = crecv[step, group, k, pl.ds(n, 1), :] * inside
            return carry

        lax.fori_loop(0, count, one, 0)

    def turn(t):
        drain(in_recv.at[t], (PARTS - 1) * 2 * SHARE)
        for half in range(2):
            block = flat[t, half].T
            for i in range(4):
                ext[0, t, pl.ds((FIRST + 4 * half + i) * ROW, WY), :] = block[i * WY:(i + 1) * WY]

    def currents(step):
        def one(row, c):
            at = pl.multiple_of(row * ROW, 8)
            top = DOPPLER * jnp.tanh(ext[step, OT, pl.ds(at, ROW), :])
            tu[pl.ds(at, ROW), :] = jnp.broadcast_to(top[:, 0:1], (ROW, 128))
            tv[pl.ds(at, ROW), :] = jnp.broadcast_to(top[:, 1:2], (ROW, 128))
            return c
        lax.fori_loop(1, ROWS, one, 0)

    u_at = lambda at: tu[pl.ds(at, 16), :]
    v_at = lambda at: tv[pl.ds(at, 16), :]

    def advance(cx, cy, e_at, here, sea_here):
        new = e_at(here) * (1.0 - jnp.abs(cx + u_at(here)) - jnp.abs(cy + v_at(here)))
        new += jnp.maximum(cx + u_at(here - ROW), 0.0) * e_at(here - ROW)
        new -= jnp.minimum(cx + u_at(here + ROW), 0.0) * e_at(here + ROW)
        new += jnp.maximum(cy + v_at(here - 1), 0.0) * e_at(here - 1)
        new -= jnp.minimum(cy + v_at(here + 1), 0.0) * e_at(here + 1)
        return new * sea_here

    def advect(step, first_tile, count):
        def speeds(t):
            return jnp.concatenate([cg[0, t]] * 2, axis=0), jnp.concatenate([cg[1, t]] * 2, axis=0)

        def first(i, c):
            at = pl.multiple_of(i * 16, 16)
            sea_here = sea_ext[pl.ds(at, 16), :]
            for n in range(count):
                t = first_tile + n
                cx, cy = speeds(t)
                e1[pl.ds(pl.multiple_of(t * EXT + at, 8), 16), :] = advance(cx, cy, lambda a: ext[step, t, pl.ds(a, 16), :], at, sea_here)
            return c

        lax.fori_loop(2 * ROW // 16, 12 * ROW // 16, first, 0)

        def second(i, c):
            at = pl.multiple_of(own_row(lax.div(i, 2)) + lax.rem(i, 2) * 16, 8)
            to = pl.ds(pl.multiple_of(i * 16, 16), 16)
            sea_here = sea_ext[pl.ds(at, 16), :]
            squares = total[to, :]
            for n in range(count):
                t = first_tile + n
                cx, cy = speeds(t)
                new = advance(cx, cy, lambda a: e1[pl.ds(t * EXT + a, 16), :], at, sea_here)
                e2[t, to, :] = new
                square = new * new
                squares += square
                rounded[to, tile_rows(t)] = new.astype(jnp.bfloat16)
                squared[to, tile_rows(t)] = square.astype(jnp.bfloat16)
            total[to, :] = squares
            return c

        lax.fori_loop(0, COLS // 16, second, 0)

    def weigh():
        def one(x, c):
            to = pl.ds(pl.multiple_of(x * WY, WY), WY)
            sums = jnp.sum(total[to, :], axis=1, keepdims=True)
            weight[to, :] = sea_ext[pl.ds(own_row(x), WY), :] * (DT_SOURCE / (1.0 + sums / NB))
            return c
        lax.fori_loop(0, WX, one, 0)

    def prepare(v):
        for raw, out in ((kl_raw, wl), (ks_raw, ws)):
            for u in range(LT):
                block = raw[v].reshape(128, NB)[:, u * 128:(u + 1) * 128].T
                for i in range(8):
                    k, t = divmod(8 * u + i, LT)
                    out[pl.ds(128 * t + SHARE * k, SHARE), tile_rows(v)] = block[i * SHARE:(i + 1) * SHARE]

    turn(OT)
    send_halo(0, 3)

    drain(sea_recv.at[0], 2 * 16)
    drain(sea_send.at[0], 2 * 16)
    sea_turned[...] = jnp.zeros_like(sea_turned)
    for h in range(2):
        lanes = slice(h * 128, (h + 1) * 128)
        rows = jnp.concatenate(
            [sea_raw[0, :, lanes], sea_raw[1, :, lanes], sea_raw[2, :, lanes], jnp.zeros((104, 128), jnp.float32)], axis=0)
        sea_turned[pl.ds(8 + h * 128, 128), :] = rows.T
    for q in range(12):
        column = q + 6
        here = sea_turned[pl.ds(pl.multiple_of(8 + r * WY, 8), ROW), :]
        sea_ext[pl.ds((q + 1) * ROW, ROW), :] = jnp.broadcast_to(here[:, column:column + 1], (ROW, 128))
        left = sea_turned[pl.ds(6 + r * WY, 2), :]
        sea_ext[pl.ds((q + 1) * ROW - 2, 2), :] = jnp.broadcast_to(left[:, column:column + 1], (2, 128))

    pltpu.make_async_copy(dk_raw, dk_raw, weights_sem.at[0]).wait()
    for u in range(LT):
        block = dk_raw[:, u * 128:(u + 1) * 128].T
        for i in range(8):
            k, t = divmod(8 * u + i, LT)
            wd[pl.ds(128 * t + SHARE * k, SHARE), :] = block[i * SHARE:(i + 1) * SHARE]

    def advect_pairs(step, group):
        take_halo(step, group)
        begin, count = GROUPS[group]

        def one(n, c):
            advect(step, 2 * n, 2)
            return c

        lax.fori_loop(begin // 2, (begin + count) // 2, one, 0)

    def wake(step):
        take_halo(step, 3)
        currents(step)
        total[...] = jnp.zeros_like(total)

    pltpu.make_async_copy(kl_raw, kl_raw, weights_sem.at[1]).wait()
    pltpu.make_async_copy(ks_raw, ks_raw, weights_sem.at[2]).wait()

    def enter_tile(t, c):
        turn(t)

        @pl.when(t == 3)
        def _():
            send_halo(0, 0)

        @pl.when(t == 7)
        def _():
            send_halo(0, 1)

        prepare(t)

        @pl.when(t == 5)
        def _():
            wake(0)
            advect_pairs(0, 0)

        return c

    lax.fori_loop(0, LT, enter_tile, 0)
    send_halo(0, 2)
    advect_pairs(0, 1)
    take_halo(0, 2)
    advect(0, LT - 1, 1)

    lane_row = lax.broadcasted_iota(jnp.int32, (WY, 128), 1)
    even = lax.rem(lane_row, 2) == 0
    sign = jnp.where(even, DT_OCEAN, -DT_OCEAN)

    def turn_back(t, value):
        for half in range(2):
            back[t, half] = value[half * 128:(half + 1) * 128].T
        for copy in exit_copies(t):
            copy.start()
        for half in range(2):
            got[t, r, half] = back[t, half, share_rows(r), :]

    def source(step, first_tile, count, last):
        lanes = pl.ds(pl.multiple_of(first_tile * 128, 128), count * 128)
        inter = jnp.dot(rounded[...], wl[:, lanes], preferred_element_type=jnp.float32)
        inter += jnp.dot(squared[...], ws[:, lanes], preferred_element_type=jnp.float32)
        fresh = []
        for k in range(count):
            old = e2[first_tile + k]
            new = old + inter[:, k * 128:(k + 1) * 128] * old * weight[...]
            if last:
                turn_back(first_tile + k, new)
            else:
                for x in range(WX):
                    ext[step + 1, first_tile + k, pl.ds((FIRST + x) * ROW, WY), :] = new[x * WY:(x + 1) * WY]
            fresh.append(new.astype(jnp.bfloat16))
        fresh = jnp.concatenate(fresh, axis=1) if count > 1 else fresh[0]
        drift[...] += jnp.dot(fresh, wd[lanes, :], preferred_element_type=jnp.float32)

    def swim(step, last):
        def one(x, c):
            at = own_row(x)
            old = ext[step, OT, pl.ds(at, WY), :]
            lap = (ext[step, OT, pl.ds(at + ROW, WY), :] + ext[step, OT, pl.ds(at - ROW, WY), :]
                   + (ext[step, OT, pl.ds(at + 1, WY), :] + ext[step, OT, pl.ds(at - 1, WY), :]) - 4.0 * old)
            here = pl.ds(pl.multiple_of(x * WY, WY), WY)
            pushed = old + drift[here, :]
            other = jnp.where(even, pltpu.roll(pushed, 127, 1), pltpu.roll(pushed, 1, 1))
            new = (old + (sign * other + DT_OCEAN * lap)) * sea_ext[pl.ds(at, WY), :]
            if last:
                drift[here, :] = new
            else:
                ext[step + 1, OT, pl.ds(at, WY), :] = new
            return c
        lax.fori_loop(0, WX, one, 0)
        if last:
            turn_back(OT, drift[...])

    def react(step, last):
        weigh()
        drift[...] = jnp.zeros_like(drift)

        def source_pair(n, c):
            source(step, 2 * n, 2, last)
            if not last:
                @pl.when(n == 1)
                def _():
                    send_halo(step + 1, 0)
            return c

        lax.fori_loop(0, LT // 2, source_pair, 0)
        source(step, LT - 1, 1, last)
        swim(step, last)

    def whole_step(step, c):
        react(step, False)
        for group in (3, 1, 2):
            send_halo(step + 1, group)
        wake(step + 1)
        advect_pairs(step + 1, 0)
        advect_pairs(step + 1, 1)
        take_halo(step + 1, 2)
        advect(step + 1, LT - 1, 1)
        return c

    lax.fori_loop(0, STEPS - 1, whole_step, 0)
    react(STEPS - 1, True)

    def leave(t, carry):
        drain(out_recv.at[t], (PARTS - 1) * 2 * SHARE)
        for octet in range(2):
            for h in range(2):
                for half in range(2):
                    blocks = swap_blocks([got[t, 4 * h + j, half, pl.ds(octet * 8, 8), :] for j in range(4)])
                    for i in range(4):
                        spec_out[h, pl.ds(t * 128 + octet * 64 + 4 * half + i, 8, stride=8), :] = blocks[i]
        for h in range(2):
            pltpu.make_async_copy(
                spec_out.at[h, tile_rows(t)], eo.at[tile_rows(t), half_lanes(h)], store.at[0]).start()
        return carry

    lax.fori_loop(0, LT, leave, 0)
    drain(out_recv.at[OT], (PARTS - 1) * 2 * SHARE)
    for comp in range(2):
        for h in range(2):
            for half in range(2):
                blocks = swap_blocks([got[OT, 4 * h + j, half, pl.ds(comp, 8, stride=2), :] for j in range(4)])
                for i in range(4):
                    swim_out[h, pl.ds(64 * comp + 4 * half + i, 8, stride=8), :] = blocks[i]
    for h in range(2):
        pltpu.make_async_copy(swim_out.at[h], oo.at[:, half_lanes(h)], store.at[0]).start()
    drain(store.at[0], 2 * NB + 256)
    drain(in_send.at[0], NT * (PARTS - 1) * 2 * SHARE)
    drain(out_send.at[0], NT * (PARTS - 1) * 2 * SHARE)
    for step in range(STEPS):
        drain(halo_send.at[step], NT * (4 * WY + 2 * SMALL) + len(GROUPS) * 4 * 8)


def per_device(spectrum, sea_mask, kernel_linear, kernel_square, drift_kernel, ocean):
    y = spectrum.shape[2]
    any_ = pl.BlockSpec(memory_space=pl.ANY)
    vmem = pl.BlockSpec(memory_space=pltpu.VMEM)
    f32, bf16 = jnp.float32, jnp.bfloat16
    dma = pltpu.SemaphoreType.DMA
    eo, oo = pl.pallas_call(
        kernel,
        out_shape=(jax.ShapeDtypeStruct((NB, y), f32), jax.ShapeDtypeStruct((128, y), f32)),
        in_specs=[any_, any_, vmem, any_, any_, any_, vmem],
        out_specs=(any_, any_),
        scratch_shapes=[
            pltpu.VMEM((2, NB, 128), f32),
            pltpu.VMEM((2, 128, 128), f32),
            pltpu.VMEM((NT, PARTS, 2, SHARE, 128), f32),
            pltpu.VMEM((NT, 2, 128, 128), f32),
            pltpu.VMEM((STEPS, NT, EXT, 128), f32),
            pltpu.VMEM((3, 8, y), f32),
            pltpu.VMEM((8 + 256 + ROW, 128), f32),
            pltpu.VMEM((EXT, 128), f32),
            pltpu.VMEM((LT * EXT, 128), f32),
            pltpu.VMEM((LT, COLS, 128), f32),
            pltpu.VMEM((COLS, NB), bf16),
            pltpu.VMEM((COLS, NB), bf16),
            pltpu.VMEM((EXT, 128), f32),
            pltpu.VMEM((EXT, 128), f32),
            pltpu.VMEM((COLS, 128), f32),
            pltpu.VMEM((COLS, 128), f32),
            pltpu.VMEM((COLS, 128), f32),
            pltpu.VMEM((LT, PARTS, SHARE, NB), bf16),
            pltpu.VMEM((LT, PARTS, SHARE, NB), bf16),
            pltpu.VMEM((128, NB), bf16),
            pltpu.VMEM((NB, NB), bf16),
            pltpu.VMEM((NB, NB), bf16),
            pltpu.VMEM((NB, 128), bf16),
            pltpu.VMEM((STEPS, 2, NT, 2, WX, 128), f32),
            pltpu.VMEM((STEPS, 2, NT, 2, WX, 128), f32),
            pltpu.VMEM((STEPS, len(GROUPS), 4, 8, 128), f32),
            pltpu.VMEM((STEPS, len(GROUPS), 4, 8, 128), f32),
            pltpu.VMEM((NT, 2, 128, 128), f32),
            pltpu.VMEM((NT, PARTS, 2, SHARE, 128), f32),
            pltpu.VMEM((2, NB, 128), f32),
            pltpu.VMEM((2, 128, 128), f32),
            dma((1,)),
            dma((NT,)),
            dma((STEPS,)),
            dma((STEPS, len(GROUPS))),
            dma((1,)),
            dma((1,)),
            dma((1,)),
            dma((NT,)),
            dma((NT,)),
            dma((3,)),
            dma((1,)),
        ],
        compiler_params=pltpu.CompilerParams(
            collective_id=0, has_side_effects=True, vmem_limit_bytes=60 * 1024 * 1024
        ),
        name="coupled",
    )(
        spectrum.reshape(NB, y),
        ocean.reshape(128, y),
        sea_mask,
        kernel_linear.reshape(PARTS, LT, SHARE, NB),
        kernel_square.reshape(PARTS, LT, SHARE, NB),
        drift_kernel,
        jnp.asarray(group_speeds()),
    )
    return eo.reshape(spectrum.shape), oo.reshape(ocean.shape)


def solution(mesh):
    return jax.shard_map(
        per_device,
        mesh=mesh,
        in_specs=(
            P("bins", "geo", None),
            P("geo", None),
            P(),
            P(),
            P(),
            P(None, "bins", "geo", None),
        ),
        out_specs=(P("bins", "geo", None), P(None, "bins", "geo", None)),
        check_vma=False,
    )
```

```python
import jax
import jax.numpy as jnp
import numpy as np
from jax import lax
from jax.experimental import pallas as pl
from jax.experimental.pallas import tpu as pltpu
from jax.sharding import PartitionSpec as P

NDIR = 36
NFREQ = 32
NB = 1152
STEPS = 3
PARTS = 8
BINS = NB // PARTS
SHARE = 16
WX = 8
WY = 32
COLS = WX * WY
LT = NB // 128
OT = LT
NT = LT + 1
PAIRS = LT // 2
SIDES = ((0, 4), (4, 4), (LT - 1, 1), (OT, 1))
OCEAN = len(SIDES) - 1
SMALL = WX * 2
ROW = 40
ROWS = 13
EXT = ROW * ROWS
FIRST = 3
INSIDE = (FIRST + 1) * ROW
OUTSIDE = (FIRST + WX - 2) * ROW + 24

DT_SOURCE = 0.5
DT_OCEAN = 0.2
DOPPLER = 0.1

MESH = pl.DeviceIdType.MESH


def bin_order():
    return np.arange(NB).reshape(PARTS, LT, SHARE).transpose(1, 0, 2).reshape(NB)


def group_speeds():
    index = bin_order()
    direction = (index // NFREQ).astype(np.float32)
    frequency = (index % NFREQ).astype(np.float32)
    speed = np.float32(0.4) / (np.float32(1.0) + frequency / np.float32(16.0))
    angle = np.float32(2.0 * np.pi / NDIR) * direction
    both = np.stack([speed * np.cos(angle), speed * np.sin(angle)]).astype(np.float32)
    return np.ascontiguousarray(np.broadcast_to(both.reshape(2, LT, 1, 128), (2, LT, 8, 128)))


def own_row(x):
    return pl.multiple_of((FIRST + x) * ROW, 8)


def tile_rows(t):
    return pl.ds(pl.multiple_of(t * 128, 128), 128)


def share_rows(k):
    return pl.ds(pl.multiple_of(k * SHARE, SHARE), SHARE)


def kernel(
    spectrum, ocean, sea, kl, ks, dk, cg, eo, oo,
    spec, swim_in, send, flat, ext, sea_raw, sea_turned, sea_ext, e1, e2, rounded, squared, tu, tv, total, weight,
    drift, kl_raw, ks_raw, dk_raw, wl, ws, wd, ysend, yrecv, csend, crecv, back, got, spec_out, swim_out,
    in_send, in_recv, halo_send, halo_recv, sea_send, sea_recv, out_send, out_recv, load, weights_sem, store,
):
    g = lax.axis_index("geo")
    r = lax.axis_index("bins")
    tiles = lax.axis_size("geo")
    west, east = lax.rem(g + tiles - 1, tiles), lax.rem(g + 1, tiles)
    south, north = lax.rem(r + PARTS - 1, PARTS), lax.rem(r + 1, PARTS)

    barrier = pltpu.get_barrier_semaphore()
    friends = [(g, lax.rem(r + d, PARTS)) for d in range(1, PARTS)]
    friends += [(x, y) for x in (west, east) for y in (south, r, north)]
    for friend in friends:
        pl.semaphore_signal(barrier, inc=1, device_id=friend, device_id_type=MESH)

    def half_lanes(h):
        return pl.ds(h * 128, 128)

    def drain(sem, rows):
        pltpu.make_async_copy(e1.at[pl.ds(0, rows)], e1.at[pl.ds(0, rows)], sem).wait()

    def spec_load(t, c):
        for h in range(2):
            pltpu.make_async_copy(
                spectrum.at[tile_rows(t), half_lanes(h)], spec.at[h, tile_rows(t)], load.at[t]).start()
        return c

    for h in range(2):
        pltpu.make_async_copy(ocean.at[:, half_lanes(h)], swim_in.at[h], load.at[LT]).start()
    lax.fori_loop(0, LT, spec_load, 0)

    lane = lax.broadcasted_iota(jnp.int32, (8, 128), 1)
    low_half = lane < 64
    even_block = lax.rem(lax.div(lane, 32), 2) == 0

    def swap_blocks(a):
        c = [None] * 4
        for i in range(2):
            c[i] = jnp.where(low_half, a[i], pltpu.roll(a[i + 2], 64, 1))
            c[i + 2] = jnp.where(low_half, pltpu.roll(a[i], 64, 1), a[i + 2])
        out = []
        for i in (0, 2):
            out.append(jnp.where(even_block, c[i], pltpu.roll(c[i + 1], 32, 1)))
            out.append(jnp.where(even_block, pltpu.roll(c[i], 96, 1), c[i + 1]))
        return out

    def remote(src, dst, send_sem, recv_sem, device):
        return pltpu.make_async_remote_copy(
            src_ref=src, dst_ref=dst, send_sem=send_sem, recv_sem=recv_sem, device_id=device, device_id_type=MESH
        )

    def entry_copies(t):
        copies = []
        for d in range(1, PARTS):
            peer = lax.rem(r + d, PARTS)
            copies.append(remote(
                send.at[t, peer], flat.at[t, :, share_rows(r)], in_send.at[0], in_recv.at[t], (g, peer)))
        return copies

    def exit_copies(t):
        copies = []
        for d in range(1, PARTS):
            peer = lax.rem(r + d, PARTS)
            copies.append(remote(
                back.at[t, :, share_rows(peer)], got.at[t, r], out_send.at[0], out_recv.at[t], (g, peer)))
        return copies

    def ship(t):
        for copy in entry_copies(t):
            copy.start()
        for half in range(2):
            flat[t, half, share_rows(r), :] = send[t, r, half]

    sea_raw[1] = sea[...].astype(jnp.float32)
    sea_copies = [
        remote(sea_raw.at[1], sea_raw.at[2], sea_send.at[0], sea_recv.at[0], (west, r)),
        remote(sea_raw.at[1], sea_raw.at[0], sea_send.at[0], sea_recv.at[0], (east, r)),
    ]

    drain(load.at[LT], 256)
    for comp in range(2):
        for h in range(2):
            for half in range(2):
                blocks = swap_blocks(
                    [swim_in[h, pl.ds(64 * comp + 4 * half + i, 8, stride=8), :] for i in range(4)])
                for j in range(4):
                    send[OT, 4 * h + j, half, pl.ds(comp, 8, stride=2), :] = blocks[j]

    pl.semaphore_wait(barrier, len(friends))
    for copy in sea_copies:
        copy.start()
    ship(OT)

    def enter(t, carry):
        drain(load.at[t], 256)
        for octet in range(2):
            for h in range(2):
                for half in range(2):
                    blocks = swap_blocks([
                        spec[h, pl.ds(t * 128 + octet * 64 + 4 * half + i, 8, stride=8), :] for i in range(4)])
                    for j in range(4):
                        send[t, 4 * h + j, half, pl.ds(octet * 8, 8), :] = blocks[j]
        ship(t)
        return carry

    lax.fori_loop(0, LT, enter, 0)

    def weights_load(t, c):
        pltpu.make_async_copy(kl.at[:, t], kl_raw.at[t], weights_sem.at[1]).start()
        pltpu.make_async_copy(ks.at[:, t], ks_raw.at[t], weights_sem.at[2]).start()
        return c

    pltpu.make_async_copy(dk, dk_raw, weights_sem.at[0]).start()
    lax.fori_loop(0, LT, weights_load, 0)

    def rows_arrived(step, pair):
        return halo_recv.at[step, pair]

    def columns_arrived(step, group):
        return halo_recv.at[step, PAIRS + 1 + group]

    def corners_arrived(step, group):
        return halo_recv.at[step, PAIRS + 1 + len(SIDES) + group]

    def send_rows(step, first_tile, count, arrived):
        field = ext.at[step]
        every = pl.ds(first_tile, count)
        for i in range(2):
            remote(
                field.at[every, pl.ds((FIRST + i) * ROW, WY)],
                field.at[every, pl.ds((FIRST + WX + i) * ROW, WY)],
                halo_send.at[step], arrived, (west, r)).start()
            remote(
                field.at[every, pl.ds((FIRST + WX - 2 + i) * ROW, WY)],
                field.at[every, pl.ds((FIRST - 2 + i) * ROW, WY)],
                halo_send.at[step], arrived, (east, r)).start()

    corners_from = [FIRST * ROW, FIRST * ROW + WY - 1, (FIRST + WX - 1) * ROW, (FIRST + WX - 1) * ROW + WY - 1]
    corners_to = [(FIRST - 1) * ROW - 1, (FIRST - 1) * ROW + WY, (FIRST + WX) * ROW - 1, (FIRST + WX) * ROW + WY]
    has_south = (r > 0).astype(jnp.float32)
    has_north = (r < PARTS - 1).astype(jnp.float32)

    def send_sides(step, group):
        first_tile, count = SIDES[group]

        def one(n, carry):
            t = first_tile + n
            for side, start in enumerate((0, WY - 2)):
                for i in range(2):
                    ysend[step, side, t, i] = ext[step, t, pl.ds(FIRST * ROW + start + i, WX, stride=ROW), :]
            for k in range(4):
                csend[step, group, k, pl.ds(n, 1), :] = ext[step, t, pl.ds(corners_from[k], 1), :]
            return carry

        lax.fori_loop(0, count, one, 0)
        every = pl.ds(first_tile, count)
        columns, corners = columns_arrived(step, group), corners_arrived(step, group)
        ys, yr = ysend.at[step], yrecv.at[step]
        cs, cr = csend.at[step, group], crecv.at[step, group]
        for src, dst, arrived, device in (
            (ys.at[0, every], yr.at[1, every], columns, (g, south)),
            (ys.at[1, every], yr.at[0, every], columns, (g, north)),
            (cs.at[0], cr.at[3], corners, (west, south)),
            (cs.at[1], cr.at[2], corners, (west, north)),
            (cs.at[2], cr.at[1], corners, (east, south)),
            (cs.at[3], cr.at[0], corners, (east, north)),
        ):
            remote(src, dst, halo_send.at[step], arrived, device).start()

    def take_rows(step, pair, count):
        drain(rows_arrived(step, pair), count * 4 * WY)

    def take_columns(step, group):
        first_tile, count = SIDES[group]
        drain(columns_arrived(step, group), count * 2 * SMALL)

        def one(n, carry):
            t = first_tile + n
            for i in range(2):
                ext[step, t, pl.ds(FIRST * ROW - 2 + i, WX, stride=ROW), :] = yrecv[step, 0, t, i] * has_south
                ext[step, t, pl.ds(FIRST * ROW + WY + i, WX, stride=ROW), :] = yrecv[step, 1, t, i] * has_north
            return carry

        lax.fori_loop(0, count, one, 0)

    def take_corners(step, group):
        first_tile, count = SIDES[group]
        drain(corners_arrived(step, group), 4 * 8 + (4 * WY if group == OCEAN else 0))

        def one(n, carry):
            t = first_tile + n
            for k in range(4):
                inside = has_south if k % 2 == 0 else has_north
                ext[step, t, pl.ds(corners_to[k], 1), :] = crecv[step, group, k, pl.ds(n, 1), :] * inside
            return carry

        lax.fori_loop(0, count, one, 0)

    def send_ocean(step):
        send_sides(step, OCEAN)
        send_rows(step, OT, 1, corners_arrived(step, OCEAN))

    def turn(t):
        drain(in_recv.at[t], (PARTS - 1) * 2 * SHARE)
        for half in range(2):
            block = flat[t, half].T
            for i in range(4):
                ext[0, t, pl.ds((FIRST + 4 * half + i) * ROW, WY), :] = block[i * WY:(i + 1) * WY]

    def current(step, at, size):
        top = DOPPLER * jnp.tanh(ext[step, OT, pl.ds(at, size), :])
        tu[pl.ds(at, size), :] = jnp.broadcast_to(top[:, 0:1], (size, 128))
        tv[pl.ds(at, size), :] = jnp.broadcast_to(top[:, 1:2], (size, 128))

    def own_currents(step):
        def one(x, c):
            current(step, own_row(x), WY)
            return c
        lax.fori_loop(0, WX, one, 0)

    def column_currents(step):
        take_columns(step, OCEAN)

        def one(x, c):
            current(step, pl.multiple_of(own_row(x) + WY, 8), ROW - WY)
            return c
        lax.fori_loop(0, WX - 1, one, 0)

    def row_currents(step):
        take_corners(step, OCEAN)
        for row in (1, 2, FIRST + WX, FIRST + WX + 1):
            current(step, row * ROW, ROW)
        current(step, (FIRST + WX - 1) * ROW + WY, ROW - WY)

    u_at = lambda at: tu[pl.ds(at, 16), :]
    v_at = lambda at: tv[pl.ds(at, 16), :]

    def advance(cx, cy, e_at, here, sea_here):
        new = e_at(here) * (1.0 - jnp.abs(cx + u_at(here)) - jnp.abs(cy + v_at(here)))
        new += jnp.maximum(cx + u_at(here - ROW), 0.0) * e_at(here - ROW)
        new -= jnp.minimum(cx + u_at(here + ROW), 0.0) * e_at(here + ROW)
        new += jnp.maximum(cy + v_at(here - 1), 0.0) * e_at(here - 1)
        new -= jnp.minimum(cy + v_at(here + 1), 0.0) * e_at(here + 1)
        return new * sea_here

    def speeds(t):
        return jnp.concatenate([cg[0, t]] * 2, axis=0), jnp.concatenate([cg[1, t]] * 2, axis=0)

    def first_substep(step, first_tile, count, start, stop):
        def first(i, c):
            at = pl.multiple_of(i * 16, 16)
            sea_here = sea_ext[pl.ds(at, 16), :]
            for n in range(count):
                t = first_tile + n
                cx, cy = speeds(t)
                e1[pl.ds(pl.multiple_of(t * EXT + at, 8), 16), :] = advance(
                    cx, cy, lambda a: ext[step, t, pl.ds(a, 16), :], at, sea_here)
            return c

        lax.fori_loop(start // 16, stop // 16, first, 0)

    def advect_inside(step, first_tile, count):
        first_substep(step, first_tile, count, INSIDE, OUTSIDE)

    def advect(step, first_tile, count):
        first_substep(step, first_tile, count, 2 * ROW, INSIDE)
        first_substep(step, first_tile, count, OUTSIDE, 12 * ROW)

        def second(i, c):
            at = pl.multiple_of(own_row(lax.div(i, 2)) + lax.rem(i, 2) * 16, 8)
            to = pl.ds(pl.multiple_of(i * 16, 16), 16)
            sea_here = sea_ext[pl.ds(at, 16), :]
            squares = total[to, :]
            for n in range(count):
                t = first_tile + n
                cx, cy = speeds(t)
                new = advance(cx, cy, lambda a: e1[pl.ds(t * EXT + a, 16), :], at, sea_here)
                e2[t, to, :] = new
                square = new * new
                squares += square
                rounded[to, tile_rows(t)] = new.astype(jnp.bfloat16)
                squared[to, tile_rows(t)] = square.astype(jnp.bfloat16)
            total[to, :] = squares
            return c

        lax.fori_loop(0, COLS // 16, second, 0)

    def weigh():
        def one(x, c):
            to = pl.ds(pl.multiple_of(x * WY, WY), WY)
            sums = jnp.sum(total[to, :], axis=1, keepdims=True)
            weight[to, :] = sea_ext[pl.ds(own_row(x), WY), :] * (DT_SOURCE / (1.0 + sums / NB))
            return c
        lax.fori_loop(0, WX, one, 0)

    def prepare(v):
        for raw, out in ((kl_raw, wl), (ks_raw, ws)):
            for u in range(LT):
                block = raw[v].reshape(128, NB)[:, u * 128:(u + 1) * 128].T
                for i in range(8):
                    k, t = divmod(8 * u + i, LT)
                    out[pl.ds(128 * t + SHARE * k, SHARE), tile_rows(v)] = block[i * SHARE:(i + 1) * SHARE]

    turn(OT)
    send_ocean(0)
    own_currents(0)

    drain(sea_recv.at[0], 2 * 16)
    drain(sea_send.at[0], 2 * 16)
    sea_turned[...] = jnp.zeros_like(sea_turned)
    for h in range(2):
        lanes = slice(h * 128, (h + 1) * 128)
        rows = jnp.concatenate(
            [sea_raw[0, :, lanes], sea_raw[1, :, lanes], sea_raw[2, :, lanes], jnp.zeros((104, 128), jnp.float32)], axis=0)
        sea_turned[pl.ds(8 + h * 128, 128), :] = rows.T
    for q in range(12):
        column = q + 6
        here = sea_turned[pl.ds(pl.multiple_of(8 + r * WY, 8), ROW), :]
        sea_ext[pl.ds((q + 1) * ROW, ROW), :] = jnp.broadcast_to(here[:, column:column + 1], (ROW, 128))
        left = sea_turned[pl.ds(6 + r * WY, 2), :]
        sea_ext[pl.ds((q + 1) * ROW - 2, 2), :] = jnp.broadcast_to(left[:, column:column + 1], (2, 128))

    pltpu.make_async_copy(dk_raw, dk_raw, weights_sem.at[0]).wait()
    for u in range(LT):
        block = dk_raw[:, u * 128:(u + 1) * 128].T
        for i in range(8):
            k, t = divmod(8 * u + i, LT)
            wd[pl.ds(128 * t + SHARE * k, SHARE), :] = block[i * SHARE:(i + 1) * SHARE]

    def inside_pairs(step, begin, end):
        def one(n, c):
            advect_inside(step, 2 * n, 2)
            return c
        lax.fori_loop(begin, end, one, 0)

    def advect_pairs(step, begin, end):
        def one(n, c):
            take_rows(step, n, 2)
            advect(step, 2 * n, 2)
            return c
        lax.fori_loop(begin, end, one, 0)

    def advect_last(step):
        take_rows(step, PAIRS, 1)
        advect(step, LT - 1, 1)

    pltpu.make_async_copy(kl_raw, kl_raw, weights_sem.at[1]).wait()
    pltpu.make_async_copy(ks_raw, ks_raw, weights_sem.at[2]).wait()

    def enter_tile(t, c):
        prepare(t)
        turn(t)

        @pl.when(lax.rem(t, 2) == 1)
        def _():
            send_rows(0, t - 1, 2, rows_arrived(0, lax.div(t, 2)))

        @pl.when(t == 3)
        def _():
            send_sides(0, 0)

        @pl.when(t == 7)
        def _():
            send_sides(0, 1)

        @pl.when(t == 5)
        def _():
            column_currents(0)
            take_columns(0, 0)
            inside_pairs(0, 0, 2)
            row_currents(0)
            take_corners(0, 0)
            advect_pairs(0, 0, 2)

        return c

    total[...] = jnp.zeros_like(total)
    lax.fori_loop(0, LT, enter_tile, 0)
    send_sides(0, 2)
    send_rows(0, LT - 1, 1, rows_arrived(0, PAIRS))
    take_columns(0, 1)
    inside_pairs(0, 2, PAIRS)
    take_corners(0, 1)
    advect_pairs(0, 2, PAIRS)
    take_columns(0, 2)
    advect_inside(0, LT - 1, 1)
    take_corners(0, 2)
    advect_last(0)

    lane_row = lax.broadcasted_iota(jnp.int32, (WY, 128), 1)
    even = lax.rem(lane_row, 2) == 0
    sign = jnp.where(even, DT_OCEAN, -DT_OCEAN)

    def turn_back(t, value):
        for half in range(2):
            back[t, half] = value[half * 128:(half + 1) * 128].T
        for copy in exit_copies(t):
            copy.start()
        for half in range(2):
            got[t, r, half] = back[t, half, share_rows(r), :]

    def source(step, first_tile, count, last):
        lanes = pl.ds(pl.multiple_of(first_tile * 128, 128), count * 128)
        inter = jnp.dot(rounded[...], wl[:, lanes], preferred_element_type=jnp.float32)
        inter += jnp.dot(squared[...], ws[:, lanes], preferred_element_type=jnp.float32)
        fresh = []
        for k in range(count):
            old = e2[first_tile + k]
            new = old + inter[:, k * 128:(k + 1) * 128] * old * weight[...]
            if last:
                turn_back(first_tile + k, new)
            else:
                for x in range(WX):
                    ext[step + 1, first_tile + k, pl.ds((FIRST + x) * ROW, WY), :] = new[x * WY:(x + 1) * WY]
            fresh.append(new.astype(jnp.bfloat16))
        fresh = jnp.concatenate(fresh, axis=1) if count > 1 else fresh[0]
        drift[...] += jnp.dot(fresh, wd[lanes, :], preferred_element_type=jnp.float32)

    def swim(step, last):
        def one(x, c):
            at = own_row(x)
            old = ext[step, OT, pl.ds(at, WY), :]
            lap = (ext[step, OT, pl.ds(at + ROW, WY), :] + ext[step, OT, pl.ds(at - ROW, WY), :]
                   + (ext[step, OT, pl.ds(at + 1, WY), :] + ext[step, OT, pl.ds(at - 1, WY), :]) - 4.0 * old)
            here = pl.ds(pl.multiple_of(x * WY, WY), WY)
            pushed = old + drift[here, :]
            other = jnp.where(even, pltpu.roll(pushed, 127, 1), pltpu.roll(pushed, 1, 1))
            new = (old + (sign * other + DT_OCEAN * lap)) * sea_ext[pl.ds(at, WY), :]
            if last:
                drift[here, :] = new
            else:
                ext[step + 1, OT, pl.ds(at, WY), :] = new
            return c
        lax.fori_loop(0, WX, one, 0)
        if last:
            turn_back(OT, drift[...])

    def react(step, last):
        weigh()
        drift[...] = jnp.zeros_like(drift)

        def source_pair(n, c):
            source(step, 2 * n, 2, last)
            if not last:
                @pl.when(n < 2)
                def _():
                    send_rows(step + 1, 2 * n, 2, rows_arrived(step + 1, n))

                @pl.when(n == 1)
                def _():
                    send_sides(step + 1, 0)
            return c

        lax.fori_loop(0, LT // 2, source_pair, 0)
        source(step, LT - 1, 1, last)
        swim(step, last)

    def whole_step(step, c):
        react(step, False)
        send_ocean(step + 1)
        send_sides(step + 1, 1)
        send_sides(step + 1, 2)
        for n in range(2, PAIRS):
            send_rows(step + 1, 2 * n, 2, rows_arrived(step + 1, n))
        send_rows(step + 1, LT - 1, 1, rows_arrived(step + 1, PAIRS))
        later = step + 1
        own_currents(later)
        column_currents(later)
        total[...] = jnp.zeros_like(total)
        for group in range(OCEAN):
            take_columns(later, group)
        inside_pairs(later, 0, PAIRS)
        advect_inside(later, LT - 1, 1)
        row_currents(later)
        for group in range(OCEAN):
            take_corners(later, group)
        advect_pairs(later, 0, PAIRS)
        advect_last(later)
        return c

    lax.fori_loop(0, STEPS - 1, whole_step, 0)
    react(STEPS - 1, True)

    def leave(t, carry):
        drain(out_recv.at[t], (PARTS - 1) * 2 * SHARE)
        for octet in range(2):
            for h in range(2):
                for half in range(2):
                    blocks = swap_blocks([got[t, 4 * h + j, half, pl.ds(octet * 8, 8), :] for j in range(4)])
                    for i in range(4):
                        spec_out[h, pl.ds(t * 128 + octet * 64 + 4 * half + i, 8, stride=8), :] = blocks[i]
        for h in range(2):
            pltpu.make_async_copy(
                spec_out.at[h, tile_rows(t)], eo.at[tile_rows(t), half_lanes(h)], store.at[0]).start()
        return carry

    lax.fori_loop(0, LT, leave, 0)
    drain(out_recv.at[OT], (PARTS - 1) * 2 * SHARE)
    for comp in range(2):
        for h in range(2):
            for half in range(2):
                blocks = swap_blocks([got[OT, 4 * h + j, half, pl.ds(comp, 8, stride=2), :] for j in range(4)])
                for i in range(4):
                    swim_out[h, pl.ds(64 * comp + 4 * half + i, 8, stride=8), :] = blocks[i]
    for h in range(2):
        pltpu.make_async_copy(swim_out.at[h], oo.at[:, half_lanes(h)], store.at[0]).start()
    drain(store.at[0], 2 * NB + 256)
    drain(in_send.at[0], NT * (PARTS - 1) * 2 * SHARE)
    drain(out_send.at[0], NT * (PARTS - 1) * 2 * SHARE)
    for step in range(STEPS):
        drain(halo_send.at[step], NT * (4 * WY + 2 * SMALL) + len(SIDES) * 4 * 8)


def per_device(spectrum, sea_mask, kernel_linear, kernel_square, drift_kernel, ocean):
    y = spectrum.shape[2]
    any_ = pl.BlockSpec(memory_space=pl.ANY)
    vmem = pl.BlockSpec(memory_space=pltpu.VMEM)
    f32, bf16 = jnp.float32, jnp.bfloat16
    dma = pltpu.SemaphoreType.DMA
    eo, oo = pl.pallas_call(
        kernel,
        out_shape=(jax.ShapeDtypeStruct((NB, y), f32), jax.ShapeDtypeStruct((128, y), f32)),
        in_specs=[any_, any_, vmem, any_, any_, any_, vmem],
        out_specs=(any_, any_),
        scratch_shapes=[
            pltpu.VMEM((2, NB, 128), f32),
            pltpu.VMEM((2, 128, 128), f32),
            pltpu.VMEM((NT, PARTS, 2, SHARE, 128), f32),
            pltpu.VMEM((NT, 2, 128, 128), f32),
            pltpu.VMEM((STEPS, NT, EXT, 128), f32),
            pltpu.VMEM((3, 8, y), f32),
            pltpu.VMEM((8 + 256 + ROW, 128), f32),
            pltpu.VMEM((EXT, 128), f32),
            pltpu.VMEM((LT * EXT, 128), f32),
            pltpu.VMEM((LT, COLS, 128), f32),
            pltpu.VMEM((COLS, NB), bf16),
            pltpu.VMEM((COLS, NB), bf16),
            pltpu.VMEM((EXT, 128), f32),
            pltpu.VMEM((EXT, 128), f32),
            pltpu.VMEM((COLS, 128), f32),
            pltpu.VMEM((COLS, 128), f32),
            pltpu.VMEM((COLS, 128), f32),
            pltpu.VMEM((LT, PARTS, SHARE, NB), bf16),
            pltpu.VMEM((LT, PARTS, SHARE, NB), bf16),
            pltpu.VMEM((128, NB), bf16),
            pltpu.VMEM((NB, NB), bf16),
            pltpu.VMEM((NB, NB), bf16),
            pltpu.VMEM((NB, 128), bf16),
            pltpu.VMEM((STEPS, 2, NT, 2, WX, 128), f32),
            pltpu.VMEM((STEPS, 2, NT, 2, WX, 128), f32),
            pltpu.VMEM((STEPS, len(SIDES), 4, 8, 128), f32),
            pltpu.VMEM((STEPS, len(SIDES), 4, 8, 128), f32),
            pltpu.VMEM((NT, 2, 128, 128), f32),
            pltpu.VMEM((NT, PARTS, 2, SHARE, 128), f32),
            pltpu.VMEM((2, NB, 128), f32),
            pltpu.VMEM((2, 128, 128), f32),
            dma((1,)),
            dma((NT,)),
            dma((STEPS,)),
            dma((STEPS, PAIRS + 1 + 2 * len(SIDES))),
            dma((1,)),
            dma((1,)),
            dma((1,)),
            dma((NT,)),
            dma((NT,)),
            dma((3,)),
            dma((1,)),
        ],
        compiler_params=pltpu.CompilerParams(
            collective_id=0, has_side_effects=True, vmem_limit_bytes=60 * 1024 * 1024
        ),
        name="coupled",
    )(
        spectrum.reshape(NB, y),
        ocean.reshape(128, y),
        sea_mask,
        kernel_linear.reshape(PARTS, LT, SHARE, NB),
        kernel_square.reshape(PARTS, LT, SHARE, NB),
        drift_kernel,
        jnp.asarray(group_speeds()),
    )
    return eo.reshape(spectrum.shape), oo.reshape(ocean.shape)


def solution(mesh):
    return jax.shard_map(
        per_device,
        mesh=mesh,
        in_specs=(
            P("bins", "geo", None),
            P("geo", None),
            P(),
            P(),
            P(),
            P(None, "bins", "geo", None),
        ),
        out_specs=(P("bins", "geo", None), P(None, "bins", "geo", None)),
        check_vma=False,
    )
```

```python
import jax
import jax.numpy as jnp
import numpy as np
from jax import lax
from jax.experimental import pallas as pl
from jax.experimental.pallas import tpu as pltpu
from jax.sharding import PartitionSpec as P

NDIR = 36
NFREQ = 32
NB = 1152
STEPS = 3
PARTS = 8
BINS = NB // PARTS
SHARE = 16
WX = 8
WY = 32
COLS = WX * WY
LT = NB // 128
OT = LT
NT = LT + 1
PAIRS = LT // 2
SIDES = ((0, 4), (4, 4), (LT - 1, 1), (OT, 1))
OCEAN = len(SIDES) - 1
SMALL = WX * 2
ROW = 40
ROWS = 13
EXT = ROW * ROWS
FIRST = 3
INSIDE = (FIRST + 1) * ROW
OUTSIDE = (FIRST + WX - 2) * ROW + 24

DT_SOURCE = 0.5
DT_OCEAN = 0.2
DOPPLER = 0.1

MESH = pl.DeviceIdType.MESH


def bin_order():
    return np.arange(NB).reshape(PARTS, LT, SHARE).transpose(1, 0, 2).reshape(NB)


def group_speeds():
    index = bin_order()
    direction = (index // NFREQ).astype(np.float32)
    frequency = (index % NFREQ).astype(np.float32)
    speed = np.float32(0.4) / (np.float32(1.0) + frequency / np.float32(16.0))
    angle = np.float32(2.0 * np.pi / NDIR) * direction
    both = np.stack([speed * np.cos(angle), speed * np.sin(angle)]).astype(np.float32)
    return np.ascontiguousarray(np.broadcast_to(both.reshape(2, LT, 1, 128), (2, LT, 8, 128)))


def own_row(x):
    return pl.multiple_of((FIRST + x) * ROW, 8)


def tile_rows(t):
    return pl.ds(pl.multiple_of(t * 128, 128), 128)


def share_rows(k):
    return pl.ds(pl.multiple_of(k * SHARE, SHARE), SHARE)


def kernel(
    spectrum, ocean, sea, kl, ks, dk, cg, eo, oo,
    spec, swim_in, send, flat, ext, sea_raw, sea_turned, sea_ext, e1, e2, rounded, squared, tu, tv, total, weight,
    drift, kl_raw, ks_raw, dk_raw, wl, ws, wd, ysend, yrecv, csend, crecv, back, got, spec_out, swim_out,
    in_send, in_recv, halo_send, halo_recv, sea_send, sea_recv, out_send, out_recv, load, weights_sem, store,
):
    g = lax.axis_index("geo")
    r = lax.axis_index("bins")
    tiles = lax.axis_size("geo")
    west, east = lax.rem(g + tiles - 1, tiles), lax.rem(g + 1, tiles)
    south, north = lax.rem(r + PARTS - 1, PARTS), lax.rem(r + 1, PARTS)

    barrier = pltpu.get_barrier_semaphore()
    friends = [(g, lax.rem(r + d, PARTS)) for d in range(1, PARTS)]
    friends += [(x, y) for x in (west, east) for y in (south, r, north)]
    for friend in friends:
        pl.semaphore_signal(barrier, inc=1, device_id=friend, device_id_type=MESH)

    def half_lanes(h):
        return pl.ds(h * 128, 128)

    def drain(sem, rows):
        pltpu.make_async_copy(e1.at[pl.ds(0, rows)], e1.at[pl.ds(0, rows)], sem).wait()

    def spec_load(t, c):
        for h in range(2):
            pltpu.make_async_copy(
                spectrum.at[tile_rows(t), half_lanes(h)], spec.at[h, tile_rows(t)], load.at[t]).start()
        return c

    for h in range(2):
        pltpu.make_async_copy(ocean.at[:, half_lanes(h)], swim_in.at[h], load.at[LT]).start()
    lax.fori_loop(0, LT, spec_load, 0)

    lane = lax.broadcasted_iota(jnp.int32, (8, 128), 1)
    low_half = lane < 64
    even_block = lax.rem(lax.div(lane, 32), 2) == 0

    def swap_blocks(a):
        c = [None] * 4
        for i in range(2):
            c[i] = jnp.where(low_half, a[i], pltpu.roll(a[i + 2], 64, 1))
            c[i + 2] = jnp.where(low_half, pltpu.roll(a[i], 64, 1), a[i + 2])
        out = []
        for i in (0, 2):
            out.append(jnp.where(even_block, c[i], pltpu.roll(c[i + 1], 32, 1)))
            out.append(jnp.where(even_block, pltpu.roll(c[i], 96, 1), c[i + 1]))
        return out

    def remote(src, dst, send_sem, recv_sem, device):
        return pltpu.make_async_remote_copy(
            src_ref=src, dst_ref=dst, send_sem=send_sem, recv_sem=recv_sem, device_id=device, device_id_type=MESH
        )

    def entry_copies(t):
        copies = []
        for d in range(1, PARTS):
            peer = lax.rem(r + d, PARTS)
            copies.append(remote(
                send.at[t, peer], flat.at[t, :, share_rows(r)], in_send.at[0], in_recv.at[t], (g, peer)))
        return copies

    def exit_copies(t):
        copies = []
        for d in range(1, PARTS):
            peer = lax.rem(r + d, PARTS)
            copies.append(remote(
                back.at[t, :, share_rows(peer)], got.at[t, r], out_send.at[0], out_recv.at[t], (g, peer)))
        return copies

    def ship(t):
        for copy in entry_copies(t):
            copy.start()
        for half in range(2):
            flat[t, half, share_rows(r), :] = send[t, r, half]

    sea_raw[1] = sea[...].astype(jnp.float32)
    sea_copies = [
        remote(sea_raw.at[1], sea_raw.at[2], sea_send.at[0], sea_recv.at[0], (west, r)),
        remote(sea_raw.at[1], sea_raw.at[0], sea_send.at[0], sea_recv.at[0], (east, r)),
    ]

    drain(load.at[LT], 256)
    for comp in range(2):
        for h in range(2):
            for half in range(2):
                blocks = swap_blocks(
                    [swim_in[h, pl.ds(64 * comp + 4 * half + i, 8, stride=8), :] for i in range(4)])
                for j in range(4):
                    send[OT, 4 * h + j, half, pl.ds(comp, 8, stride=2), :] = blocks[j]

    pl.semaphore_wait(barrier, len(friends))
    for copy in sea_copies:
        copy.start()
    ship(OT)

    def enter(t, carry):
        drain(load.at[t], 256)
        for octet in range(2):
            for h in range(2):
                for half in range(2):
                    blocks = swap_blocks([
                        spec[h, pl.ds(t * 128 + octet * 64 + 4 * half + i, 8, stride=8), :] for i in range(4)])
                    for j in range(4):
                        send[t, 4 * h + j, half, pl.ds(octet * 8, 8), :] = blocks[j]
        ship(t)
        return carry

    lax.fori_loop(0, LT, enter, 0)

    def weights_load(t, c):
        pltpu.make_async_copy(kl.at[:, t], kl_raw.at[t], weights_sem.at[1]).start()
        pltpu.make_async_copy(ks.at[:, t], ks_raw.at[t], weights_sem.at[2]).start()
        return c

    pltpu.make_async_copy(dk, dk_raw, weights_sem.at[0]).start()
    lax.fori_loop(0, LT, weights_load, 0)

    def rows_arrived(step, pair):
        return halo_recv.at[step, pair]

    def columns_arrived(step, group):
        return halo_recv.at[step, PAIRS + 1 + group]

    def corners_arrived(step, group):
        return halo_recv.at[step, PAIRS + 1 + len(SIDES) + group]

    def send_rows(step, first_tile, count, arrived):
        field = ext.at[step]
        every = pl.ds(first_tile, count)
        for i in range(2):
            remote(
                field.at[every, pl.ds((FIRST + i) * ROW, WY)],
                field.at[every, pl.ds((FIRST + WX + i) * ROW, WY)],
                halo_send.at[step], arrived, (west, r)).start()
            remote(
                field.at[every, pl.ds((FIRST + WX - 2 + i) * ROW, WY)],
                field.at[every, pl.ds((FIRST - 2 + i) * ROW, WY)],
                halo_send.at[step], arrived, (east, r)).start()

    corners_from = [FIRST * ROW, FIRST * ROW + WY - 1, (FIRST + WX - 1) * ROW, (FIRST + WX - 1) * ROW + WY - 1]
    corners_to = [(FIRST - 1) * ROW - 1, (FIRST - 1) * ROW + WY, (FIRST + WX) * ROW - 1, (FIRST + WX) * ROW + WY]
    has_south = (r > 0).astype(jnp.float32)
    has_north = (r < PARTS - 1).astype(jnp.float32)

    def send_sides(step, group):
        first_tile, count = SIDES[group]

        def one(n, carry):
            t = first_tile + n
            for side, start in enumerate((0, WY - 2)):
                for i in range(2):
                    ysend[step, side, t, i] = ext[step, t, pl.ds(FIRST * ROW + start + i, WX, stride=ROW), :]
            for k in range(4):
                csend[step, group, k, pl.ds(n, 1), :] = ext[step, t, pl.ds(corners_from[k], 1), :]
            return carry

        lax.fori_loop(0, count, one, 0)
        every = pl.ds(first_tile, count)
        columns, corners = columns_arrived(step, group), corners_arrived(step, group)
        ys, yr = ysend.at[step], yrecv.at[step]
        cs, cr = csend.at[step, group], crecv.at[step, group]
        for src, dst, arrived, device in (
            (ys.at[0, every], yr.at[1, every], columns, (g, south)),
            (ys.at[1, every], yr.at[0, every], columns, (g, north)),
            (cs.at[0], cr.at[3], corners, (west, south)),
            (cs.at[1], cr.at[2], corners, (west, north)),
            (cs.at[2], cr.at[1], corners, (east, south)),
            (cs.at[3], cr.at[0], corners, (east, north)),
        ):
            remote(src, dst, halo_send.at[step], arrived, device).start()

    def take_rows(step, pair, count):
        drain(rows_arrived(step, pair), count * 4 * WY)

    def take_columns(step, group):
        first_tile, count = SIDES[group]
        drain(columns_arrived(step, group), count * 2 * SMALL)

        def one(n, carry):
            t = first_tile + n
            for i in range(2):
                ext[step, t, pl.ds(FIRST * ROW - 2 + i, WX, stride=ROW), :] = yrecv[step, 0, t, i] * has_south
                ext[step, t, pl.ds(FIRST * ROW + WY + i, WX, stride=ROW), :] = yrecv[step, 1, t, i] * has_north
            return carry

        lax.fori_loop(0, count, one, 0)

    def take_corners(step, group):
        first_tile, count = SIDES[group]
        drain(corners_arrived(step, group), 4 * 8 + (4 * WY if group == OCEAN else 0))

        def one(n, carry):
            t = first_tile + n
            for k in range(4):
                inside = has_south if k % 2 == 0 else has_north
                ext[step, t, pl.ds(corners_to[k], 1), :] = crecv[step, group, k, pl.ds(n, 1), :] * inside
            return carry

        lax.fori_loop(0, count, one, 0)

    def send_ocean(step):
        send_sides(step, OCEAN)
        send_rows(step, OT, 1, corners_arrived(step, OCEAN))

    def turn(t):
        drain(in_recv.at[t], (PARTS - 1) * 2 * SHARE)
        for half in range(2):
            block = flat[t, half].T
            for i in range(4):
                ext[0, t, pl.ds((FIRST + 4 * half + i) * ROW, WY), :] = block[i * WY:(i + 1) * WY]

    def current(step, at, size):
        top = DOPPLER * jnp.tanh(ext[step, OT, pl.ds(at, size), :])
        tu[pl.ds(at, size), :] = jnp.broadcast_to(top[:, 0:1], (size, 128))
        tv[pl.ds(at, size), :] = jnp.broadcast_to(top[:, 1:2], (size, 128))

    def own_currents(step):
        def one(x, c):
            current(step, own_row(x), WY)
            return c
        lax.fori_loop(0, WX, one, 0)

    def column_currents(step):
        take_columns(step, OCEAN)

        def one(x, c):
            current(step, pl.multiple_of(own_row(x) + WY, 8), ROW - WY)
            return c
        lax.fori_loop(0, WX - 1, one, 0)

    def row_currents(step):
        take_corners(step, OCEAN)
        for row in (1, 2, FIRST + WX, FIRST + WX + 1):
            current(step, row * ROW, ROW)
        current(step, (FIRST + WX - 1) * ROW + WY, ROW - WY)

    u_at = lambda at: tu[pl.ds(at, 16), :]
    v_at = lambda at: tv[pl.ds(at, 16), :]

    def advance(cx, cy, e_at, here, sea_here):
        new = e_at(here) * (1.0 - jnp.abs(cx + u_at(here)) - jnp.abs(cy + v_at(here)))
        new += jnp.maximum(cx + u_at(here - ROW), 0.0) * e_at(here - ROW)
        new -= jnp.minimum(cx + u_at(here + ROW), 0.0) * e_at(here + ROW)
        new += jnp.maximum(cy + v_at(here - 1), 0.0) * e_at(here - 1)
        new -= jnp.minimum(cy + v_at(here + 1), 0.0) * e_at(here + 1)
        return new * sea_here

    def speeds(t):
        return jnp.concatenate([cg[0, t]] * 2, axis=0), jnp.concatenate([cg[1, t]] * 2, axis=0)

    def first_substep(step, first_tile, count, start, stop):
        def first(i, c):
            at = pl.multiple_of(i * 16, 16)
            sea_here = sea_ext[pl.ds(at, 16), :]
            for n in range(count):
                t = first_tile + n
                cx, cy = speeds(t)
                e1[pl.ds(pl.multiple_of(t * EXT + at, 8), 16), :] = advance(
                    cx, cy, lambda a: ext[step, t, pl.ds(a, 16), :], at, sea_here)
            return c

        lax.fori_loop(start // 16, stop // 16, first, 0)

    def advect_inside(step, first_tile, count):
        first_substep(step, first_tile, count, INSIDE, OUTSIDE)

    def advect(step, first_tile, count):
        first_substep(step, first_tile, count, 2 * ROW, INSIDE)
        first_substep(step, first_tile, count, OUTSIDE, 12 * ROW)

        def second(i, c):
            at = pl.multiple_of(own_row(lax.div(i, 2)) + lax.rem(i, 2) * 16, 8)
            to = pl.ds(pl.multiple_of(i * 16, 16), 16)
            sea_here = sea_ext[pl.ds(at, 16), :]
            squares = total[to, :]
            for n in range(count):
                t = first_tile + n
                cx, cy = speeds(t)
                new = advance(cx, cy, lambda a: e1[pl.ds(t * EXT + a, 16), :], at, sea_here)
                e2[t, to, :] = new
                square = new * new
                squares += square
                rounded[to, tile_rows(t)] = new.astype(jnp.bfloat16)
                squared[to, tile_rows(t)] = square.astype(jnp.bfloat16)
            total[to, :] = squares
            return c

        lax.fori_loop(0, COLS // 16, second, 0)

    def weigh():
        def one(x, c):
            to = pl.ds(pl.multiple_of(x * WY, WY), WY)
            sums = jnp.sum(total[to, :], axis=1, keepdims=True)
            weight[to, :] = sea_ext[pl.ds(own_row(x), WY), :] * (DT_SOURCE / (1.0 + sums / NB))
            return c
        lax.fori_loop(0, WX, one, 0)

    def prepare(v):
        for raw, out in ((kl_raw, wl), (ks_raw, ws)):
            for u in range(LT):
                block = raw[v].reshape(128, NB)[:, u * 128:(u + 1) * 128].T
                for i in range(8):
                    k, t = divmod(8 * u + i, LT)
                    out[pl.ds(128 * t + SHARE * k, SHARE), tile_rows(v)] = block[i * SHARE:(i + 1) * SHARE]

    turn(OT)
    send_ocean(0)
    own_currents(0)

    drain(sea_recv.at[0], 2 * 16)
    drain(sea_send.at[0], 2 * 16)
    sea_turned[...] = jnp.zeros_like(sea_turned)
    for h in range(2):
        lanes = slice(h * 128, (h + 1) * 128)
        rows = jnp.concatenate(
            [sea_raw[0, :, lanes], sea_raw[1, :, lanes], sea_raw[2, :, lanes], jnp.zeros((104, 128), jnp.float32)], axis=0)
        sea_turned[pl.ds(8 + h * 128, 128), :] = rows.T
    for q in range(12):
        column = q + 6
        here = sea_turned[pl.ds(pl.multiple_of(8 + r * WY, 8), ROW), :]
        sea_ext[pl.ds((q + 1) * ROW, ROW), :] = jnp.broadcast_to(here[:, column:column + 1], (ROW, 128))
        left = sea_turned[pl.ds(6 + r * WY, 2), :]
        sea_ext[pl.ds((q + 1) * ROW - 2, 2), :] = jnp.broadcast_to(left[:, column:column + 1], (2, 128))

    pltpu.make_async_copy(dk_raw, dk_raw, weights_sem.at[0]).wait()
    for u in range(LT):
        block = dk_raw[:, u * 128:(u + 1) * 128].T
        for i in range(8):
            k, t = divmod(8 * u + i, LT)
            wd[pl.ds(128 * t + SHARE * k, SHARE), :] = block[i * SHARE:(i + 1) * SHARE]

    def inside_pairs(step, begin, end):
        def one(n, c):
            advect_inside(step, 2 * n, 2)
            return c
        lax.fori_loop(begin, end, one, 0)

    def advect_pairs(step, begin, end):
        def one(n, c):
            take_rows(step, n, 2)
            advect(step, 2 * n, 2)
            return c
        lax.fori_loop(begin, end, one, 0)

    def advect_last(step):
        take_rows(step, PAIRS, 1)
        advect(step, LT - 1, 1)

    pltpu.make_async_copy(kl_raw, kl_raw, weights_sem.at[1]).wait()
    pltpu.make_async_copy(ks_raw, ks_raw, weights_sem.at[2]).wait()

    def enter_tile(t, c):
        prepare(t)
        turn(t)

        @pl.when(lax.rem(t, 2) == 1)
        def _():
            send_rows(0, t - 1, 2, rows_arrived(0, lax.div(t, 2)))

        @pl.when(t == 3)
        def _():
            send_sides(0, 0)

        @pl.when(t == 7)
        def _():
            send_sides(0, 1)

        return c

    total[...] = jnp.zeros_like(total)
    lax.fori_loop(0, LT, enter_tile, 0)
    send_sides(0, 2)
    send_rows(0, LT - 1, 1, rows_arrived(0, PAIRS))
    column_currents(0)
    take_columns(0, 0)
    inside_pairs(0, 0, 2)
    row_currents(0)
    take_corners(0, 0)
    advect_pairs(0, 0, 2)
    take_columns(0, 1)
    inside_pairs(0, 2, PAIRS)
    take_corners(0, 1)
    advect_pairs(0, 2, PAIRS)
    take_columns(0, 2)
    advect_inside(0, LT - 1, 1)
    take_corners(0, 2)
    advect_last(0)

    lane_row = lax.broadcasted_iota(jnp.int32, (WY, 128), 1)
    even = lax.rem(lane_row, 2) == 0
    sign = jnp.where(even, DT_OCEAN, -DT_OCEAN)

    def turn_back(t, value):
        for half in range(2):
            back[t, half] = value[half * 128:(half + 1) * 128].T
        for copy in exit_copies(t):
            copy.start()
        for half in range(2):
            got[t, r, half] = back[t, half, share_rows(r), :]

    def source(step, first_tile, count, last):
        lanes = pl.ds(pl.multiple_of(first_tile * 128, 128), count * 128)
        inter = jnp.dot(rounded[...], wl[:, lanes], preferred_element_type=jnp.float32)
        inter += jnp.dot(squared[...], ws[:, lanes], preferred_element_type=jnp.float32)
        fresh = []
        for k in range(count):
            old = e2[first_tile + k]
            new = old + inter[:, k * 128:(k + 1) * 128] * old * weight[...]
            if last:
                turn_back(first_tile + k, new)
            else:
                for x in range(WX):
                    ext[step + 1, first_tile + k, pl.ds((FIRST + x) * ROW, WY), :] = new[x * WY:(x + 1) * WY]
            fresh.append(new.astype(jnp.bfloat16))
        fresh = jnp.concatenate(fresh, axis=1) if count > 1 else fresh[0]
        drift[...] += jnp.dot(fresh, wd[lanes, :], preferred_element_type=jnp.float32)

    def swim(step, last):
        def one(x, c):
            at = own_row(x)
            old = ext[step, OT, pl.ds(at, WY), :]
            lap = (ext[step, OT, pl.ds(at + ROW, WY), :] + ext[step, OT, pl.ds(at - ROW, WY), :]
                   + (ext[step, OT, pl.ds(at + 1, WY), :] + ext[step, OT, pl.ds(at - 1, WY), :]) - 4.0 * old)
            here = pl.ds(pl.multiple_of(x * WY, WY), WY)
            pushed = old + drift[here, :]
            other = jnp.where(even, pltpu.roll(pushed, 127, 1), pltpu.roll(pushed, 1, 1))
            new = (old + (sign * other + DT_OCEAN * lap)) * sea_ext[pl.ds(at, WY), :]
            if last:
                drift[here, :] = new
            else:
                ext[step + 1, OT, pl.ds(at, WY), :] = new
            return c
        lax.fori_loop(0, WX, one, 0)
        if last:
            turn_back(OT, drift[...])

    def react(step, last):
        weigh()
        drift[...] = jnp.zeros_like(drift)

        def source_pair(n, c):
            source(step, 2 * n, 2, last)
            if not last:
                @pl.when(n < 2)
                def _():
                    send_rows(step + 1, 2 * n, 2, rows_arrived(step + 1, n))

                @pl.when(n == 1)
                def _():
                    send_sides(step + 1, 0)
            return c

        lax.fori_loop(0, LT // 2, source_pair, 0)
        source(step, LT - 1, 1, last)
        swim(step, last)

    def whole_step(step, c):
        react(step, False)
        send_ocean(step + 1)
        send_sides(step + 1, 1)
        send_sides(step + 1, 2)
        for n in range(2, PAIRS):
            send_rows(step + 1, 2 * n, 2, rows_arrived(step + 1, n))
        send_rows(step + 1, LT - 1, 1, rows_arrived(step + 1, PAIRS))
        later = step + 1
        own_currents(later)
        column_currents(later)
        total[...] = jnp.zeros_like(total)
        for group in range(OCEAN):
            take_columns(later, group)
        inside_pairs(later, 0, PAIRS)
        advect_inside(later, LT - 1, 1)
        row_currents(later)
        for group in range(OCEAN):
            take_corners(later, group)
        advect_pairs(later, 0, PAIRS)
        advect_last(later)
        return c

    lax.fori_loop(0, STEPS - 1, whole_step, 0)
    react(STEPS - 1, True)

    def leave(t, carry):
        drain(out_recv.at[t], (PARTS - 1) * 2 * SHARE)
        for octet in range(2):
            for h in range(2):
                for half in range(2):
                    blocks = swap_blocks([got[t, 4 * h + j, half, pl.ds(octet * 8, 8), :] for j in range(4)])
                    for i in range(4):
                        spec_out[h, pl.ds(t * 128 + octet * 64 + 4 * half + i, 8, stride=8), :] = blocks[i]
        for h in range(2):
            pltpu.make_async_copy(
                spec_out.at[h, tile_rows(t)], eo.at[tile_rows(t), half_lanes(h)], store.at[0]).start()
        return carry

    lax.fori_loop(0, LT, leave, 0)
    drain(out_recv.at[OT], (PARTS - 1) * 2 * SHARE)
    for comp in range(2):
        for h in range(2):
            for half in range(2):
                blocks = swap_blocks([got[OT, 4 * h + j, half, pl.ds(comp, 8, stride=2), :] for j in range(4)])
                for i in range(4):
                    swim_out[h, pl.ds(64 * comp + 4 * half + i, 8, stride=8), :] = blocks[i]
    for h in range(2):
        pltpu.make_async_copy(swim_out.at[h], oo.at[:, half_lanes(h)], store.at[0]).start()
    drain(store.at[0], 2 * NB + 256)
    drain(in_send.at[0], NT * (PARTS - 1) * 2 * SHARE)
    drain(out_send.at[0], NT * (PARTS - 1) * 2 * SHARE)
    for step in range(STEPS):
        drain(halo_send.at[step], NT * (4 * WY + 2 * SMALL) + len(SIDES) * 4 * 8)


def per_device(spectrum, sea_mask, kernel_linear, kernel_square, drift_kernel, ocean):
    y = spectrum.shape[2]
    any_ = pl.BlockSpec(memory_space=pl.ANY)
    vmem = pl.BlockSpec(memory_space=pltpu.VMEM)
    f32, bf16 = jnp.float32, jnp.bfloat16
    dma = pltpu.SemaphoreType.DMA
    eo, oo = pl.pallas_call(
        kernel,
        out_shape=(jax.ShapeDtypeStruct((NB, y), f32), jax.ShapeDtypeStruct((128, y), f32)),
        in_specs=[any_, any_, vmem, any_, any_, any_, vmem],
        out_specs=(any_, any_),
        scratch_shapes=[
            pltpu.VMEM((2, NB, 128), f32),
            pltpu.VMEM((2, 128, 128), f32),
            pltpu.VMEM((NT, PARTS, 2, SHARE, 128), f32),
            pltpu.VMEM((NT, 2, 128, 128), f32),
            pltpu.VMEM((STEPS, NT, EXT, 128), f32),
            pltpu.VMEM((3, 8, y), f32),
            pltpu.VMEM((8 + 256 + ROW, 128), f32),
            pltpu.VMEM((EXT, 128), f32),
            pltpu.VMEM((LT * EXT, 128), f32),
            pltpu.VMEM((LT, COLS, 128), f32),
            pltpu.VMEM((COLS, NB), bf16),
            pltpu.VMEM((COLS, NB), bf16),
            pltpu.VMEM((EXT, 128), f32),
            pltpu.VMEM((EXT, 128), f32),
            pltpu.VMEM((COLS, 128), f32),
            pltpu.VMEM((COLS, 128), f32),
            pltpu.VMEM((COLS, 128), f32),
            pltpu.VMEM((LT, PARTS, SHARE, NB), bf16),
            pltpu.VMEM((LT, PARTS, SHARE, NB), bf16),
            pltpu.VMEM((128, NB), bf16),
            pltpu.VMEM((NB, NB), bf16),
            pltpu.VMEM((NB, NB), bf16),
            pltpu.VMEM((NB, 128), bf16),
            pltpu.VMEM((STEPS, 2, NT, 2, WX, 128), f32),
            pltpu.VMEM((STEPS, 2, NT, 2, WX, 128), f32),
            pltpu.VMEM((STEPS, len(SIDES), 4, 8, 128), f32),
            pltpu.VMEM((STEPS, len(SIDES), 4, 8, 128), f32),
            pltpu.VMEM((NT, 2, 128, 128), f32),
            pltpu.VMEM((NT, PARTS, 2, SHARE, 128), f32),
            pltpu.VMEM((2, NB, 128), f32),
            pltpu.VMEM((2, 128, 128), f32),
            dma((1,)),
            dma((NT,)),
            dma((STEPS,)),
            dma((STEPS, PAIRS + 1 + 2 * len(SIDES))),
            dma((1,)),
            dma((1,)),
            dma((1,)),
            dma((NT,)),
            dma((NT,)),
            dma((3,)),
            dma((1,)),
        ],
        compiler_params=pltpu.CompilerParams(
            collective_id=0, has_side_effects=True, vmem_limit_bytes=60 * 1024 * 1024
        ),
        name="coupled",
    )(
        spectrum.reshape(NB, y),
        ocean.reshape(128, y),
        sea_mask,
        kernel_linear.reshape(PARTS, LT, SHARE, NB),
        kernel_square.reshape(PARTS, LT, SHARE, NB),
        drift_kernel,
        jnp.asarray(group_speeds()),
    )
    return eo.reshape(spectrum.shape), oo.reshape(ocean.shape)


def solution(mesh):
    return jax.shard_map(
        per_device,
        mesh=mesh,
        in_specs=(
            P("bins", "geo", None),
            P("geo", None),
            P(),
            P(),
            P(),
            P(None, "bins", "geo", None),
        ),
        out_specs=(P("bins", "geo", None), P(None, "bins", "geo", None)),
        check_vma=False,
    )
```

```python
import jax
import jax.numpy as jnp
import numpy as np
from jax import lax
from jax.experimental import pallas as pl
from jax.experimental.pallas import tpu as pltpu
from jax.sharding import PartitionSpec as P

NDIR = 36
NFREQ = 32
NB = 1152
STEPS = 3
PARTS = 8
BINS = NB // PARTS
SHARE = 16
WX = 8
WY = 32
COLS = WX * WY
LT = NB // 128
OT = LT
NT = LT + 1
PAIRS = LT // 2
SIDES = ((0, 4), (4, 4), (LT - 1, 1), (OT, 1))
OCEAN = len(SIDES) - 1
SMALL = WX * 2
ROW = 40
ROWS = 13
EXT = ROW * ROWS
FIRST = 3
INSIDE = (FIRST + 1) * ROW
OUTSIDE = (FIRST + WX - 2) * ROW + 24

DT_SOURCE = 0.5
DT_OCEAN = 0.2
DOPPLER = 0.1

MESH = pl.DeviceIdType.MESH


def bin_order():
    return np.arange(NB).reshape(PARTS, LT, SHARE).transpose(1, 0, 2).reshape(NB)


def group_speeds():
    index = bin_order()
    direction = (index // NFREQ).astype(np.float32)
    frequency = (index % NFREQ).astype(np.float32)
    speed = np.float32(0.4) / (np.float32(1.0) + frequency / np.float32(16.0))
    angle = np.float32(2.0 * np.pi / NDIR) * direction
    both = np.stack([speed * np.cos(angle), speed * np.sin(angle)]).astype(np.float32)
    return np.ascontiguousarray(np.broadcast_to(both.reshape(2, LT, 1, 128), (2, LT, 8, 128)))


def own_row(x):
    return pl.multiple_of((FIRST + x) * ROW, 8)


def tile_rows(t):
    return pl.ds(pl.multiple_of(t * 128, 128), 128)


def share_rows(k):
    return pl.ds(pl.multiple_of(k * SHARE, SHARE), SHARE)


def kernel(
    spectrum, ocean, sea, kl, ks, dk, cg, eo, oo,
    spec, swim_in, send, flat, ext, sea_raw, sea_turned, sea_ext, e1, e2, rounded, squared, tu, tv, total, weight,
    drift, kl_raw, ks_raw, dk_raw, wl, ws, wd, ysend, yrecv, csend, crecv, back, got, spec_out, swim_out,
    in_send, in_recv, halo_send, halo_recv, sea_send, sea_recv, out_send, out_recv, load, weights_sem, store,
):
    g = lax.axis_index("geo")
    r = lax.axis_index("bins")
    tiles = lax.axis_size("geo")
    west, east = lax.rem(g + tiles - 1, tiles), lax.rem(g + 1, tiles)
    south, north = lax.rem(r + PARTS - 1, PARTS), lax.rem(r + 1, PARTS)

    barrier = pltpu.get_barrier_semaphore()
    friends = [(g, lax.rem(r + d, PARTS)) for d in range(1, PARTS)]
    friends += [(x, y) for x in (west, east) for y in (south, r, north)]
    for friend in friends:
        pl.semaphore_signal(barrier, inc=1, device_id=friend, device_id_type=MESH)

    def half_lanes(h):
        return pl.ds(h * 128, 128)

    def drain(sem, rows):
        pltpu.make_async_copy(e1.at[pl.ds(0, rows)], e1.at[pl.ds(0, rows)], sem).wait()

    def spec_load(t, c):
        for h in range(2):
            pltpu.make_async_copy(
                spectrum.at[tile_rows(t), half_lanes(h)], spec.at[h, tile_rows(t)], load.at[t]).start()
        return c

    for h in range(2):
        pltpu.make_async_copy(ocean.at[:, half_lanes(h)], swim_in.at[h], load.at[LT]).start()
    lax.fori_loop(0, LT, spec_load, 0)

    lane = lax.broadcasted_iota(jnp.int32, (8, 128), 1)
    low_half = lane < 64
    even_block = lax.rem(lax.div(lane, 32), 2) == 0

    def swap_blocks(a):
        c = [None] * 4
        for i in range(2):
            c[i] = jnp.where(low_half, a[i], pltpu.roll(a[i + 2], 64, 1))
            c[i + 2] = jnp.where(low_half, pltpu.roll(a[i], 64, 1), a[i + 2])
        out = []
        for i in (0, 2):
            out.append(jnp.where(even_block, c[i], pltpu.roll(c[i + 1], 32, 1)))
            out.append(jnp.where(even_block, pltpu.roll(c[i], 96, 1), c[i + 1]))
        return out

    def remote(src, dst, send_sem, recv_sem, device):
        return pltpu.make_async_remote_copy(
            src_ref=src, dst_ref=dst, send_sem=send_sem, recv_sem=recv_sem, device_id=device, device_id_type=MESH
        )

    def entry_copies(t):
        copies = []
        for d in range(1, PARTS):
            peer = lax.rem(r + d, PARTS)
            copies.append(remote(
                send.at[t, peer], flat.at[t, :, share_rows(r)], in_send.at[0], in_recv.at[t], (g, peer)))
        return copies

    def exit_copies(t):
        copies = []
        for d in range(1, PARTS):
            peer = lax.rem(r + d, PARTS)
            copies.append(remote(
                back.at[t, :, share_rows(peer)], got.at[t, r], out_send.at[0], out_recv.at[t], (g, peer)))
        return copies

    def ship(t):
        for copy in entry_copies(t):
            copy.start()
        for half in range(2):
            flat[t, half, share_rows(r), :] = send[t, r, half]

    sea_raw[1] = sea[...].astype(jnp.float32)
    sea_copies = [
        remote(sea_raw.at[1], sea_raw.at[2], sea_send.at[0], sea_recv.at[0], (west, r)),
        remote(sea_raw.at[1], sea_raw.at[0], sea_send.at[0], sea_recv.at[0], (east, r)),
    ]

    drain(load.at[LT], 256)
    for comp in range(2):
        for h in range(2):
            for half in range(2):
                blocks = swap_blocks(
                    [swim_in[h, pl.ds(64 * comp + 4 * half + i, 8, stride=8), :] for i in range(4)])
                for j in range(4):
                    send[OT, 4 * h + j, half, pl.ds(comp, 8, stride=2), :] = blocks[j]

    pl.semaphore_wait(barrier, len(friends))
    for copy in sea_copies:
        copy.start()
    ship(OT)

    def enter(t, carry):
        drain(load.at[t], 256)
        for octet in range(2):
            for h in range(2):
                for half in range(2):
                    blocks = swap_blocks([
                        spec[h, pl.ds(t * 128 + octet * 64 + 4 * half + i, 8, stride=8), :] for i in range(4)])
                    for j in range(4):
                        send[t, 4 * h + j, half, pl.ds(octet * 8, 8), :] = blocks[j]
        ship(t)
        return carry

    lax.fori_loop(0, LT, enter, 0)

    def weights_load(t, c):
        pltpu.make_async_copy(kl.at[:, t], kl_raw.at[t], weights_sem.at[1]).start()
        pltpu.make_async_copy(ks.at[:, t], ks_raw.at[t], weights_sem.at[2]).start()
        return c

    pltpu.make_async_copy(dk, dk_raw, weights_sem.at[0]).start()
    lax.fori_loop(0, LT, weights_load, 0)

    def rows_arrived(step, pair):
        return halo_recv.at[step, pair]

    def columns_arrived(step, group):
        return halo_recv.at[step, PAIRS + 1 + group]

    def corners_arrived(step, group):
        return halo_recv.at[step, PAIRS + 1 + len(SIDES) + group]

    def send_rows(step, first_tile, count, arrived):
        field = ext.at[step]
        every = pl.ds(first_tile, count)
        for i in range(2):
            remote(
                field.at[every, pl.ds((FIRST + i) * ROW, WY)],
                field.at[every, pl.ds((FIRST + WX + i) * ROW, WY)],
                halo_send.at[step], arrived, (west, r)).start()
            remote(
                field.at[every, pl.ds((FIRST + WX - 2 + i) * ROW, WY)],
                field.at[every, pl.ds((FIRST - 2 + i) * ROW, WY)],
                halo_send.at[step], arrived, (east, r)).start()

    corners_from = [FIRST * ROW, FIRST * ROW + WY - 1, (FIRST + WX - 1) * ROW, (FIRST + WX - 1) * ROW + WY - 1]
    corners_to = [(FIRST - 1) * ROW - 1, (FIRST - 1) * ROW + WY, (FIRST + WX) * ROW - 1, (FIRST + WX) * ROW + WY]
    has_south = (r > 0).astype(jnp.float32)
    has_north = (r < PARTS - 1).astype(jnp.float32)

    def send_sides(step, group):
        first_tile, count = SIDES[group]

        def one(n, carry):
            t = first_tile + n
            for side, start in enumerate((0, WY - 2)):
                for i in range(2):
                    ysend[step, side, t, i] = ext[step, t, pl.ds(FIRST * ROW + start + i, WX, stride=ROW), :]
            for k in range(4):
                csend[step, group, k, pl.ds(n, 1), :] = ext[step, t, pl.ds(corners_from[k], 1), :]
            return carry

        lax.fori_loop(0, count, one, 0)
        every = pl.ds(first_tile, count)
        columns, corners = columns_arrived(step, group), corners_arrived(step, group)
        ys, yr = ysend.at[step], yrecv.at[step]
        cs, cr = csend.at[step, group], crecv.at[step, group]
        for src, dst, arrived, device in (
            (ys.at[0, every], yr.at[1, every], columns, (g, south)),
            (ys.at[1, every], yr.at[0, every], columns, (g, north)),
            (cs.at[0], cr.at[3], corners, (west, south)),
            (cs.at[1], cr.at[2], corners, (west, north)),
            (cs.at[2], cr.at[1], corners, (east, south)),
            (cs.at[3], cr.at[0], corners, (east, north)),
        ):
            remote(src, dst, halo_send.at[step], arrived, device).start()

    def take_rows(step, pair, count):
        drain(rows_arrived(step, pair), count * 4 * WY)

    def take_columns(step, group):
        first_tile, count = SIDES[group]
        drain(columns_arrived(step, group), count * 2 * SMALL)

        def one(n, carry):
            t = first_tile + n
            for i in range(2):
                ext[step, t, pl.ds(FIRST * ROW - 2 + i, WX, stride=ROW), :] = yrecv[step, 0, t, i] * has_south
                ext[step, t, pl.ds(FIRST * ROW + WY + i, WX, stride=ROW), :] = yrecv[step, 1, t, i] * has_north
            return carry

        lax.fori_loop(0, count, one, 0)

    def take_corners(step, group):
        first_tile, count = SIDES[group]
        drain(corners_arrived(step, group), 4 * 8 + (4 * WY if group == OCEAN else 0))

        def one(n, carry):
            t = first_tile + n
            for k in range(4):
                inside = has_south if k % 2 == 0 else has_north
                ext[step, t, pl.ds(corners_to[k], 1), :] = crecv[step, group, k, pl.ds(n, 1), :] * inside
            return carry

        lax.fori_loop(0, count, one, 0)

    def send_ocean(step):
        send_sides(step, OCEAN)
        send_rows(step, OT, 1, corners_arrived(step, OCEAN))

    def turn(t):
        drain(in_recv.at[t], (PARTS - 1) * 2 * SHARE)
        for half in range(2):
            block = flat[t, half].T
            for i in range(4):
                ext[0, t, pl.ds((FIRST + 4 * half + i) * ROW, WY), :] = block[i * WY:(i + 1) * WY]

    def current(step, at, size):
        top = DOPPLER * jnp.tanh(ext[step, OT, pl.ds(at, size), :])
        tu[pl.ds(at, size), :] = jnp.broadcast_to(top[:, 0:1], (size, 128))
        tv[pl.ds(at, size), :] = jnp.broadcast_to(top[:, 1:2], (size, 128))

    def own_currents(step):
        def one(x, c):
            current(step, own_row(x), WY)
            return c
        lax.fori_loop(0, WX, one, 0)

    def column_currents(step):
        take_columns(step, OCEAN)

        def one(x, c):
            current(step, pl.multiple_of(own_row(x) + WY, 8), ROW - WY)
            return c
        lax.fori_loop(0, WX - 1, one, 0)

    def row_currents(step):
        take_corners(step, OCEAN)
        for row in (1, 2, FIRST + WX, FIRST + WX + 1):
            current(step, row * ROW, ROW)
        current(step, (FIRST + WX - 1) * ROW + WY, ROW - WY)

    u_at = lambda at: tu[pl.ds(at, 16), :]
    v_at = lambda at: tv[pl.ds(at, 16), :]

    def advance(cx, cy, e_at, here, sea_here):
        new = e_at(here) * (1.0 - jnp.abs(cx + u_at(here)) - jnp.abs(cy + v_at(here)))
        new += jnp.maximum(cx + u_at(here - ROW), 0.0) * e_at(here - ROW)
        new -= jnp.minimum(cx + u_at(here + ROW), 0.0) * e_at(here + ROW)
        new += jnp.maximum(cy + v_at(here - 1), 0.0) * e_at(here - 1)
        new -= jnp.minimum(cy + v_at(here + 1), 0.0) * e_at(here + 1)
        return new * sea_here

    def speeds(t):
        return jnp.concatenate([cg[0, t]] * 2, axis=0), jnp.concatenate([cg[1, t]] * 2, axis=0)

    def first_substep(step, first_tile, count, start, stop):
        def first(i, c):
            at = pl.multiple_of(i * 16, 16)
            sea_here = sea_ext[pl.ds(at, 16), :]
            for n in range(count):
                t = first_tile + n
                cx, cy = speeds(t)
                e1[pl.ds(pl.multiple_of(t * EXT + at, 8), 16), :] = advance(
                    cx, cy, lambda a: ext[step, t, pl.ds(a, 16), :], at, sea_here)
            return c

        begin, times = start // 16, (stop - start) // 16
        if times % 2:
            lax.fori_loop(begin, begin + times, first, 0)
        else:
            lax.fori_loop(0, times // 2, lambda i, c: first(begin + 2 * i + 1, first(begin + 2 * i, c)), 0)

    def advect_inside(step, first_tile, count):
        first_substep(step, first_tile, count, INSIDE, OUTSIDE)

    def advect(step, first_tile, count):
        first_substep(step, first_tile, count, 2 * ROW, INSIDE)
        first_substep(step, first_tile, count, OUTSIDE, 12 * ROW)

        def second(i, c):
            at = pl.multiple_of(own_row(lax.div(i, 2)) + lax.rem(i, 2) * 16, 8)
            to = pl.ds(pl.multiple_of(i * 16, 16), 16)
            sea_here = sea_ext[pl.ds(at, 16), :]
            squares = total[to, :]
            for n in range(count):
                t = first_tile + n
                cx, cy = speeds(t)
                new = advance(cx, cy, lambda a: e1[pl.ds(t * EXT + a, 16), :], at, sea_here)
                e2[t, to, :] = new
                square = new * new
                squares += square
                rounded[to, tile_rows(t)] = new.astype(jnp.bfloat16)
                squared[to, tile_rows(t)] = square.astype(jnp.bfloat16)
            total[to, :] = squares
            return c

        def four(i, c):
            for j in range(4):
                c = second(4 * i + j, c)
            return c

        lax.fori_loop(0, COLS // 64, four, 0)

    def weigh():
        def one(x, c):
            to = pl.ds(pl.multiple_of(x * WY, WY), WY)
            sums = jnp.sum(total[to, :], axis=1, keepdims=True)
            weight[to, :] = sea_ext[pl.ds(own_row(x), WY), :] * (DT_SOURCE / (1.0 + sums / NB))
            return c
        lax.fori_loop(0, WX, one, 0)

    def prepare(v):
        for raw, out in ((kl_raw, wl), (ks_raw, ws)):
            for u in range(LT):
                block = raw[v].reshape(128, NB)[:, u * 128:(u + 1) * 128].T
                for i in range(8):
                    k, t = divmod(8 * u + i, LT)
                    out[pl.ds(128 * t + SHARE * k, SHARE), tile_rows(v)] = block[i * SHARE:(i + 1) * SHARE]

    turn(OT)
    send_ocean(0)
    own_currents(0)

    drain(sea_recv.at[0], 2 * 16)
    drain(sea_send.at[0], 2 * 16)
    sea_turned[...] = jnp.zeros_like(sea_turned)
    for h in range(2):
        lanes = slice(h * 128, (h + 1) * 128)
        rows = jnp.concatenate(
            [sea_raw[0, :, lanes], sea_raw[1, :, lanes], sea_raw[2, :, lanes], jnp.zeros((104, 128), jnp.float32)], axis=0)
        sea_turned[pl.ds(8 + h * 128, 128), :] = rows.T
    for q in range(12):
        column = q + 6
        here = sea_turned[pl.ds(pl.multiple_of(8 + r * WY, 8), ROW), :]
        sea_ext[pl.ds((q + 1) * ROW, ROW), :] = jnp.broadcast_to(here[:, column:column + 1], (ROW, 128))
        left = sea_turned[pl.ds(6 + r * WY, 2), :]
        sea_ext[pl.ds((q + 1) * ROW - 2, 2), :] = jnp.broadcast_to(left[:, column:column + 1], (2, 128))

    pltpu.make_async_copy(dk_raw, dk_raw, weights_sem.at[0]).wait()
    for u in range(LT):
        block = dk_raw[:, u * 128:(u + 1) * 128].T
        for i in range(8):
            k, t = divmod(8 * u + i, LT)
            wd[pl.ds(128 * t + SHARE * k, SHARE), :] = block[i * SHARE:(i + 1) * SHARE]

    def inside_pairs(step, begin, end):
        def one(n, c):
            advect_inside(step, 2 * n, 2)
            return c
        lax.fori_loop(begin, end, one, 0)

    def advect_pairs(step, begin, end):
        def one(n, c):
            take_rows(step, n, 2)
            advect(step, 2 * n, 2)
            return c
        lax.fori_loop(begin, end, one, 0)

    def advect_last(step):
        take_rows(step, PAIRS, 1)
        advect(step, LT - 1, 1)

    pltpu.make_async_copy(kl_raw, kl_raw, weights_sem.at[1]).wait()
    pltpu.make_async_copy(ks_raw, ks_raw, weights_sem.at[2]).wait()

    def enter_tile(t, c):
        prepare(t)
        turn(t)

        @pl.when(lax.rem(t, 2) == 1)
        def _():
            send_rows(0, t - 1, 2, rows_arrived(0, lax.div(t, 2)))

        @pl.when(t == 3)
        def _():
            send_sides(0, 0)

        @pl.when(t == 7)
        def _():
            send_sides(0, 1)

        return c

    total[...] = jnp.zeros_like(total)
    lax.fori_loop(0, LT, enter_tile, 0)
    send_sides(0, 2)
    send_rows(0, LT - 1, 1, rows_arrived(0, PAIRS))
    column_currents(0)
    take_columns(0, 0)
    inside_pairs(0, 0, 2)
    row_currents(0)
    take_corners(0, 0)
    advect_pairs(0, 0, 2)
    take_columns(0, 1)
    inside_pairs(0, 2, PAIRS)
    take_corners(0, 1)
    advect_pairs(0, 2, PAIRS)
    take_columns(0, 2)
    advect_inside(0, LT - 1, 1)
    take_corners(0, 2)
    advect_last(0)

    lane_row = lax.broadcasted_iota(jnp.int32, (WY, 128), 1)
    even = lax.rem(lane_row, 2) == 0
    sign = jnp.where(even, DT_OCEAN, -DT_OCEAN)

    def turn_back(t, value):
        for half in range(2):
            back[t, half] = value[half * 128:(half + 1) * 128].T
        for copy in exit_copies(t):
            copy.start()
        for half in range(2):
            got[t, r, half] = back[t, half, share_rows(r), :]

    def source(step, first_tile, count, last):
        lanes = pl.ds(pl.multiple_of(first_tile * 128, 128), count * 128)
        inter = jnp.dot(rounded[...], wl[:, lanes], preferred_element_type=jnp.float32)
        inter += jnp.dot(squared[...], ws[:, lanes], preferred_element_type=jnp.float32)
        fresh = []
        for k in range(count):
            old = e2[first_tile + k]
            new = old + inter[:, k * 128:(k + 1) * 128] * old * weight[...]
            if last:
                turn_back(first_tile + k, new)
            else:
                for x in range(WX):
                    ext[step + 1, first_tile + k, pl.ds((FIRST + x) * ROW, WY), :] = new[x * WY:(x + 1) * WY]
            fresh.append(new.astype(jnp.bfloat16))
        fresh = jnp.concatenate(fresh, axis=1) if count > 1 else fresh[0]
        drift[...] += jnp.dot(fresh, wd[lanes, :], preferred_element_type=jnp.float32)

    def swim(step, last):
        def one(x, c):
            at = own_row(x)
            old = ext[step, OT, pl.ds(at, WY), :]
            lap = (ext[step, OT, pl.ds(at + ROW, WY), :] + ext[step, OT, pl.ds(at - ROW, WY), :]
                   + (ext[step, OT, pl.ds(at + 1, WY), :] + ext[step, OT, pl.ds(at - 1, WY), :]) - 4.0 * old)
            here = pl.ds(pl.multiple_of(x * WY, WY), WY)
            pushed = old + drift[here, :]
            other = jnp.where(even, pltpu.roll(pushed, 127, 1), pltpu.roll(pushed, 1, 1))
            new = (old + (sign * other + DT_OCEAN * lap)) * sea_ext[pl.ds(at, WY), :]
            if last:
                drift[here, :] = new
            else:
                ext[step + 1, OT, pl.ds(at, WY), :] = new
            return c
        lax.fori_loop(0, WX, one, 0)
        if last:
            turn_back(OT, drift[...])

    def react(step, last):
        weigh()
        drift[...] = jnp.zeros_like(drift)

        def source_pair(n, c):
            source(step, 2 * n, 2, last)
            if not last:
                @pl.when(n < 2)
                def _():
                    send_rows(step + 1, 2 * n, 2, rows_arrived(step + 1, n))

                @pl.when(n == 1)
                def _():
                    send_sides(step + 1, 0)
            return c

        lax.fori_loop(0, LT // 2, source_pair, 0)
        source(step, LT - 1, 1, last)
        swim(step, last)

    def whole_step(step, c):
        react(step, False)
        send_ocean(step + 1)
        send_sides(step + 1, 1)
        send_sides(step + 1, 2)
        for n in range(2, PAIRS):
            send_rows(step + 1, 2 * n, 2, rows_arrived(step + 1, n))
        send_rows(step + 1, LT - 1, 1, rows_arrived(step + 1, PAIRS))
        later = step + 1
        own_currents(later)
        column_currents(later)
        total[...] = jnp.zeros_like(total)
        for group in range(OCEAN):
            take_columns(later, group)
        inside_pairs(later, 0, PAIRS)
        advect_inside(later, LT - 1, 1)
        row_currents(later)
        for group in range(OCEAN):
            take_corners(later, group)
        advect_pairs(later, 0, PAIRS)
        advect_last(later)
        return c

    lax.fori_loop(0, STEPS - 1, whole_step, 0)
    react(STEPS - 1, True)

    def leave(t, carry):
        drain(out_recv.at[t], (PARTS - 1) * 2 * SHARE)
        for octet in range(2):
            for h in range(2):
                for half in range(2):
                    blocks = swap_blocks([got[t, 4 * h + j, half, pl.ds(octet * 8, 8), :] for j in range(4)])
                    for i in range(4):
                        spec_out[h, pl.ds(t * 128 + octet * 64 + 4 * half + i, 8, stride=8), :] = blocks[i]
        for h in range(2):
            pltpu.make_async_copy(
                spec_out.at[h, tile_rows(t)], eo.at[tile_rows(t), half_lanes(h)], store.at[0]).start()
        return carry

    lax.fori_loop(0, LT, leave, 0)
    drain(out_recv.at[OT], (PARTS - 1) * 2 * SHARE)
    for comp in range(2):
        for h in range(2):
            for half in range(2):
                blocks = swap_blocks([got[OT, 4 * h + j, half, pl.ds(comp, 8, stride=2), :] for j in range(4)])
                for i in range(4):
                    swim_out[h, pl.ds(64 * comp + 4 * half + i, 8, stride=8), :] = blocks[i]
    for h in range(2):
        pltpu.make_async_copy(swim_out.at[h], oo.at[:, half_lanes(h)], store.at[0]).start()
    drain(store.at[0], 2 * NB + 256)
    drain(in_send.at[0], NT * (PARTS - 1) * 2 * SHARE)
    drain(out_send.at[0], NT * (PARTS - 1) * 2 * SHARE)
    for step in range(STEPS):
        drain(halo_send.at[step], NT * (4 * WY + 2 * SMALL) + len(SIDES) * 4 * 8)


def per_device(spectrum, sea_mask, kernel_linear, kernel_square, drift_kernel, ocean):
    y = spectrum.shape[2]
    any_ = pl.BlockSpec(memory_space=pl.ANY)
    vmem = pl.BlockSpec(memory_space=pltpu.VMEM)
    f32, bf16 = jnp.float32, jnp.bfloat16
    dma = pltpu.SemaphoreType.DMA
    eo, oo = pl.pallas_call(
        kernel,
        out_shape=(jax.ShapeDtypeStruct((NB, y), f32), jax.ShapeDtypeStruct((128, y), f32)),
        in_specs=[any_, any_, vmem, any_, any_, any_, vmem],
        out_specs=(any_, any_),
        scratch_shapes=[
            pltpu.VMEM((2, NB, 128), f32),
            pltpu.VMEM((2, 128, 128), f32),
            pltpu.VMEM((NT, PARTS, 2, SHARE, 128), f32),
            pltpu.VMEM((NT, 2, 128, 128), f32),
            pltpu.VMEM((STEPS, NT, EXT, 128), f32),
            pltpu.VMEM((3, 8, y), f32),
            pltpu.VMEM((8 + 256 + ROW, 128), f32),
            pltpu.VMEM((EXT, 128), f32),
            pltpu.VMEM((LT * EXT, 128), f32),
            pltpu.VMEM((LT, COLS, 128), f32),
            pltpu.VMEM((COLS, NB), bf16),
            pltpu.VMEM((COLS, NB), bf16),
            pltpu.VMEM((EXT, 128), f32),
            pltpu.VMEM((EXT, 128), f32),
            pltpu.VMEM((COLS, 128), f32),
            pltpu.VMEM((COLS, 128), f32),
            pltpu.VMEM((COLS, 128), f32),
            pltpu.VMEM((LT, PARTS, SHARE, NB), bf16),
            pltpu.VMEM((LT, PARTS, SHARE, NB), bf16),
            pltpu.VMEM((128, NB), bf16),
            pltpu.VMEM((NB, NB), bf16),
            pltpu.VMEM((NB, NB), bf16),
            pltpu.VMEM((NB, 128), bf16),
            pltpu.VMEM((STEPS, 2, NT, 2, WX, 128), f32),
            pltpu.VMEM((STEPS, 2, NT, 2, WX, 128), f32),
            pltpu.VMEM((STEPS, len(SIDES), 4, 8, 128), f32),
            pltpu.VMEM((STEPS, len(SIDES), 4, 8, 128), f32),
            pltpu.VMEM((NT, 2, 128, 128), f32),
            pltpu.VMEM((NT, PARTS, 2, SHARE, 128), f32),
            pltpu.VMEM((2, NB, 128), f32),
            pltpu.VMEM((2, 128, 128), f32),
            dma((1,)),
            dma((NT,)),
            dma((STEPS,)),
            dma((STEPS, PAIRS + 1 + 2 * len(SIDES))),
            dma((1,)),
            dma((1,)),
            dma((1,)),
            dma((NT,)),
            dma((NT,)),
            dma((3,)),
            dma((1,)),
        ],
        compiler_params=pltpu.CompilerParams(
            collective_id=0, has_side_effects=True, vmem_limit_bytes=60 * 1024 * 1024
        ),
        name="coupled",
    )(
        spectrum.reshape(NB, y),
        ocean.reshape(128, y),
        sea_mask,
        kernel_linear.reshape(PARTS, LT, SHARE, NB),
        kernel_square.reshape(PARTS, LT, SHARE, NB),
        drift_kernel,
        jnp.asarray(group_speeds()),
    )
    return eo.reshape(spectrum.shape), oo.reshape(ocean.shape)


def solution(mesh):
    return jax.shard_map(
        per_device,
        mesh=mesh,
        in_specs=(
            P("bins", "geo", None),
            P("geo", None),
            P(),
            P(),
            P(),
            P(None, "bins", "geo", None),
        ),
        out_specs=(P("bins", "geo", None), P(None, "bins", "geo", None)),
        check_vma=False,
    )
```

```python
import jax
import jax.numpy as jnp
import numpy as np
from jax import lax
from jax.experimental import pallas as pl
from jax.experimental.pallas import tpu as pltpu
from jax.sharding import PartitionSpec as P

NDIR = 36
NFREQ = 32
NB = 1152
STEPS = 3
PARTS = 8
BINS = NB // PARTS
SHARE = 16
WX = 8
WY = 32
COLS = WX * WY
LT = NB // 128
OT = LT
NT = LT + 1
PAIRS = LT // 2
SIDES = ((0, 4), (4, 4), (LT - 1, 1), (OT, 1))
OCEAN = len(SIDES) - 1
SMALL = WX * 2
ROW = 40
ROWS = 13
EXT = ROW * ROWS
FIRST = 3
INSIDE = (FIRST + 1) * ROW
OUTSIDE = (FIRST + WX - 2) * ROW + 24

DT_SOURCE = 0.5
DT_OCEAN = 0.2
DOPPLER = 0.1

MESH = pl.DeviceIdType.MESH


def bin_order():
    return np.arange(NB).reshape(PARTS, LT, SHARE).transpose(1, 0, 2).reshape(NB)


def group_speeds():
    index = bin_order()
    direction = (index // NFREQ).astype(np.float32)
    frequency = (index % NFREQ).astype(np.float32)
    speed = np.float32(0.4) / (np.float32(1.0) + frequency / np.float32(16.0))
    angle = np.float32(2.0 * np.pi / NDIR) * direction
    both = np.stack([speed * np.cos(angle), speed * np.sin(angle)]).astype(np.float32)
    return np.ascontiguousarray(np.broadcast_to(both.reshape(2, LT, 1, 128), (2, LT, 8, 128)))


def own_row(x):
    return pl.multiple_of((FIRST + x) * ROW, 8)


def tile_rows(t):
    return pl.ds(pl.multiple_of(t * 128, 128), 128)


def share_rows(k):
    return pl.ds(pl.multiple_of(k * SHARE, SHARE), SHARE)


def kernel(
    spectrum, ocean, sea, kl, ks, dk, cg, eo, oo,
    spec, swim_in, send, flat, ext, sea_raw, sea_turned, sea_ext, e1, e2, rounded, squared, tu, tv, total, weight,
    drift, kl_raw, ks_raw, dk_raw, wl, ws, wd, ysend, yrecv, csend, crecv, back, got, spec_out, swim_out,
    in_send, in_recv, halo_send, halo_recv, sea_send, sea_recv, out_send, out_recv, load, weights_sem, store,
):
    g = lax.axis_index("geo")
    r = lax.axis_index("bins")
    tiles = lax.axis_size("geo")
    west, east = lax.rem(g + tiles - 1, tiles), lax.rem(g + 1, tiles)
    south, north = lax.rem(r + PARTS - 1, PARTS), lax.rem(r + 1, PARTS)

    barrier = pltpu.get_barrier_semaphore()
    friends = [(g, lax.rem(r + d, PARTS)) for d in range(1, PARTS)]
    friends += [(x, y) for x in (west, east) for y in (south, r, north)]
    for friend in friends:
        pl.semaphore_signal(barrier, inc=1, device_id=friend, device_id_type=MESH)

    def half_lanes(h):
        return pl.ds(h * 128, 128)

    def drain(sem, rows):
        pltpu.make_async_copy(e1.at[pl.ds(0, rows)], e1.at[pl.ds(0, rows)], sem).wait()

    def spec_load(t, c):
        for h in range(2):
            pltpu.make_async_copy(
                spectrum.at[tile_rows(t), half_lanes(h)], spec.at[h, tile_rows(t)], load.at[t]).start()
        return c

    for h in range(2):
        pltpu.make_async_copy(ocean.at[:, half_lanes(h)], swim_in.at[h], load.at[LT]).start()
    lax.fori_loop(0, LT, spec_load, 0)

    lane = lax.broadcasted_iota(jnp.int32, (8, 128), 1)
    low_half = lane < 64
    even_block = lax.rem(lax.div(lane, 32), 2) == 0

    def swap_blocks(a):
        c = [None] * 4
        for i in range(2):
            c[i] = jnp.where(low_half, a[i], pltpu.roll(a[i + 2], 64, 1))
            c[i + 2] = jnp.where(low_half, pltpu.roll(a[i], 64, 1), a[i + 2])
        out = []
        for i in (0, 2):
            out.append(jnp.where(even_block, c[i], pltpu.roll(c[i + 1], 32, 1)))
            out.append(jnp.where(even_block, pltpu.roll(c[i], 96, 1), c[i + 1]))
        return out

    def remote(src, dst, send_sem, recv_sem, device):
        return pltpu.make_async_remote_copy(
            src_ref=src, dst_ref=dst, send_sem=send_sem, recv_sem=recv_sem, device_id=device, device_id_type=MESH
        )

    def entry_copies(t):
        copies = []
        for d in range(1, PARTS):
            peer = lax.rem(r + d, PARTS)
            copies.append(remote(
                send.at[t, peer], flat.at[t, :, share_rows(r)], in_send.at[0], in_recv.at[t], (g, peer)))
        return copies

    def exit_copies(t):
        copies = []
        for d in range(1, PARTS):
            peer = lax.rem(r + d, PARTS)
            copies.append(remote(
                back.at[t, :, share_rows(peer)], got.at[t, r], out_send.at[0], out_recv.at[t], (g, peer)))
        return copies

    def ship(t):
        for copy in entry_copies(t):
            copy.start()
        for half in range(2):
            flat[t, half, share_rows(r), :] = send[t, r, half]

    sea_raw[1] = sea[...].astype(jnp.float32)
    sea_copies = [
        remote(sea_raw.at[1], sea_raw.at[2], sea_send.at[0], sea_recv.at[0], (west, r)),
        remote(sea_raw.at[1], sea_raw.at[0], sea_send.at[0], sea_recv.at[0], (east, r)),
    ]

    drain(load.at[LT], 256)
    for comp in range(2):
        for h in range(2):
            for half in range(2):
                blocks = swap_blocks(
                    [swim_in[h, pl.ds(64 * comp + 4 * half + i, 8, stride=8), :] for i in range(4)])
                for j in range(4):
                    send[OT, 4 * h + j, half, pl.ds(comp, 8, stride=2), :] = blocks[j]

    pl.semaphore_wait(barrier, len(friends))
    for copy in sea_copies:
        copy.start()
    ship(OT)

    def enter(t, carry):
        drain(load.at[t], 256)
        for octet in range(2):
            for h in range(2):
                for half in range(2):
                    blocks = swap_blocks([
                        spec[h, pl.ds(t * 128 + octet * 64 + 4 * half + i, 8, stride=8), :] for i in range(4)])
                    for j in range(4):
                        send[t, 4 * h + j, half, pl.ds(octet * 8, 8), :] = blocks[j]
        ship(t)
        return carry

    lax.fori_loop(0, LT, enter, 0)

    def weights_load(t, c):
        pltpu.make_async_copy(kl.at[:, t], kl_raw.at[t], weights_sem.at[1]).start()
        pltpu.make_async_copy(ks.at[:, t], ks_raw.at[t], weights_sem.at[2]).start()
        return c

    pltpu.make_async_copy(dk, dk_raw, weights_sem.at[0]).start()
    lax.fori_loop(0, LT, weights_load, 0)

    def rows_arrived(step, pair):
        return halo_recv.at[step, pair]

    def columns_arrived(step, group):
        return halo_recv.at[step, PAIRS + 1 + group]

    def corners_arrived(step, group):
        return halo_recv.at[step, PAIRS + 1 + len(SIDES) + group]

    def send_rows(step, first_tile, count, arrived):
        field = ext.at[step]
        every = pl.ds(first_tile, count)
        for i in range(2):
            remote(
                field.at[every, pl.ds((FIRST + i) * ROW, WY)],
                field.at[every, pl.ds((FIRST + WX + i) * ROW, WY)],
                halo_send.at[step], arrived, (west, r)).start()
            remote(
                field.at[every, pl.ds((FIRST + WX - 2 + i) * ROW, WY)],
                field.at[every, pl.ds((FIRST - 2 + i) * ROW, WY)],
                halo_send.at[step], arrived, (east, r)).start()

    corners_from = [FIRST * ROW, FIRST * ROW + WY - 1, (FIRST + WX - 1) * ROW, (FIRST + WX - 1) * ROW + WY - 1]
    corners_to = [(FIRST - 1) * ROW - 1, (FIRST - 1) * ROW + WY, (FIRST + WX) * ROW - 1, (FIRST + WX) * ROW + WY]
    has_south = (r > 0).astype(jnp.float32)
    has_north = (r < PARTS - 1).astype(jnp.float32)

    def send_sides(step, group):
        first_tile, count = SIDES[group]

        def one(n, carry):
            t = first_tile + n
            for side, start in enumerate((0, WY - 2)):
                for i in range(2):
                    ysend[step, side, t, i] = ext[step, t, pl.ds(FIRST * ROW + start + i, WX, stride=ROW), :]
            for k in range(4):
                csend[step, group, k, pl.ds(n, 1), :] = ext[step, t, pl.ds(corners_from[k], 1), :]
            return carry

        lax.fori_loop(0, count, one, 0)
        every = pl.ds(first_tile, count)
        columns, corners = columns_arrived(step, group), corners_arrived(step, group)
        ys, yr = ysend.at[step], yrecv.at[step]
        cs, cr = csend.at[step, group], crecv.at[step, group]
        for src, dst, arrived, device in (
            (ys.at[0, every], yr.at[1, every], columns, (g, south)),
            (ys.at[1, every], yr.at[0, every], columns, (g, north)),
            (cs.at[0], cr.at[3], corners, (west, south)),
            (cs.at[1], cr.at[2], corners, (west, north)),
            (cs.at[2], cr.at[1], corners, (east, south)),
            (cs.at[3], cr.at[0], corners, (east, north)),
        ):
            remote(src, dst, halo_send.at[step], arrived, device).start()

    def take_rows(step, pair, count):
        drain(rows_arrived(step, pair), count * 4 * WY)

    def take_columns(step, group):
        first_tile, count = SIDES[group]
        drain(columns_arrived(step, group), count * 2 * SMALL)

        def one(n, carry):
            t = first_tile + n
            for i in range(2):
                ext[step, t, pl.ds(FIRST * ROW - 2 + i, WX, stride=ROW), :] = yrecv[step, 0, t, i] * has_south
                ext[step, t, pl.ds(FIRST * ROW + WY + i, WX, stride=ROW), :] = yrecv[step, 1, t, i] * has_north
            return carry

        lax.fori_loop(0, count, one, 0)

    def take_corners(step, group):
        first_tile, count = SIDES[group]
        drain(corners_arrived(step, group), 4 * 8 + (4 * WY if group == OCEAN else 0))

        def one(n, carry):
            t = first_tile + n
            for k in range(4):
                inside = has_south if k % 2 == 0 else has_north
                ext[step, t, pl.ds(corners_to[k], 1), :] = crecv[step, group, k, pl.ds(n, 1), :] * inside
            return carry

        lax.fori_loop(0, count, one, 0)

    def send_ocean(step):
        send_sides(step, OCEAN)
        send_rows(step, OT, 1, corners_arrived(step, OCEAN))

    def turn(t):
        drain(in_recv.at[t], (PARTS - 1) * 2 * SHARE)
        for half in range(2):
            block = flat[t, half].T
            for i in range(4):
                ext[0, t, pl.ds((FIRST + 4 * half + i) * ROW, WY), :] = block[i * WY:(i + 1) * WY]

    def current(step, at, size):
        top = DOPPLER * jnp.tanh(ext[step, OT, pl.ds(at, size), :])
        tu[pl.ds(at, size), :] = jnp.broadcast_to(top[:, 0:1], (size, 128))
        tv[pl.ds(at, size), :] = jnp.broadcast_to(top[:, 1:2], (size, 128))

    def own_currents(step):
        def one(x, c):
            current(step, own_row(x), WY)
            return c
        lax.fori_loop(0, WX, one, 0)

    def column_currents(step):
        take_columns(step, OCEAN)

        def one(x, c):
            current(step, pl.multiple_of(own_row(x) + WY, 8), ROW - WY)
            return c
        lax.fori_loop(0, WX - 1, one, 0)

    def row_currents(step):
        take_corners(step, OCEAN)
        for row in (1, 2, FIRST + WX, FIRST + WX + 1):
            current(step, row * ROW, ROW)
        current(step, (FIRST + WX - 1) * ROW + WY, ROW - WY)

    u_at = lambda at: tu[pl.ds(at, 16), :]
    v_at = lambda at: tv[pl.ds(at, 16), :]

    def advance(cx, cy, e_at, here, sea_here):
        new = e_at(here) * (1.0 - jnp.abs(cx + u_at(here)) - jnp.abs(cy + v_at(here)))
        new += jnp.maximum(cx + u_at(here - ROW), 0.0) * e_at(here - ROW)
        new -= jnp.minimum(cx + u_at(here + ROW), 0.0) * e_at(here + ROW)
        new += jnp.maximum(cy + v_at(here - 1), 0.0) * e_at(here - 1)
        new -= jnp.minimum(cy + v_at(here + 1), 0.0) * e_at(here + 1)
        return new * sea_here

    def speeds(t):
        return jnp.concatenate([cg[0, t]] * 2, axis=0), jnp.concatenate([cg[1, t]] * 2, axis=0)

    def first_substep(step, first_tile, count, start, stop):
        def first(i, c):
            at = pl.multiple_of(i * 16, 16)
            sea_here = sea_ext[pl.ds(at, 16), :]
            for n in range(count):
                t = first_tile + n
                cx, cy = speeds(t)
                e1[pl.ds(pl.multiple_of(t * EXT + at, 8), 16), :] = advance(
                    cx, cy, lambda a: ext[step, t, pl.ds(a, 16), :], at, sea_here)
            return c

        begin, times = start // 16, (stop - start) // 16
        if times % 2:
            for i in range(begin, begin + times):
                first(i, 0)
        else:
            lax.fori_loop(0, times // 2, lambda i, c: first(begin + 2 * i + 1, first(begin + 2 * i, c)), 0)

    def advect_inside(step, first_tile, count):
        first_substep(step, first_tile, count, INSIDE, OUTSIDE)

    def advect(step, first_tile, count):
        first_substep(step, first_tile, count, 2 * ROW, INSIDE)
        first_substep(step, first_tile, count, OUTSIDE, 12 * ROW)

        def second(i, c):
            at = pl.multiple_of(own_row(lax.div(i, 2)) + lax.rem(i, 2) * 16, 8)
            to = pl.ds(pl.multiple_of(i * 16, 16), 16)
            sea_here = sea_ext[pl.ds(at, 16), :]
            squares = total[to, :]
            for n in range(count):
                t = first_tile + n
                cx, cy = speeds(t)
                new = advance(cx, cy, lambda a: e1[pl.ds(t * EXT + a, 16), :], at, sea_here)
                e2[t, to, :] = new
                square = new * new
                squares += square
                rounded[to, tile_rows(t)] = new.astype(jnp.bfloat16)
                squared[to, tile_rows(t)] = square.astype(jnp.bfloat16)
            total[to, :] = squares
            return c

        def four(i, c):
            for j in range(4):
                c = second(4 * i + j, c)
            return c

        lax.fori_loop(0, COLS // 64, four, 0)

    def weigh():
        def one(x, c):
            to = pl.ds(pl.multiple_of(x * WY, WY), WY)
            sums = jnp.sum(total[to, :], axis=1, keepdims=True)
            weight[to, :] = sea_ext[pl.ds(own_row(x), WY), :] * (DT_SOURCE / (1.0 + sums / NB))
            return c
        lax.fori_loop(0, WX, one, 0)

    def prepare(v):
        for raw, out in ((kl_raw, wl), (ks_raw, ws)):
            for u in range(LT):
                block = raw[v].reshape(128, NB)[:, u * 128:(u + 1) * 128].T
                for i in range(8):
                    k, t = divmod(8 * u + i, LT)
                    out[pl.ds(128 * t + SHARE * k, SHARE), tile_rows(v)] = block[i * SHARE:(i + 1) * SHARE]

    turn(OT)
    send_ocean(0)
    own_currents(0)

    drain(sea_recv.at[0], 2 * 16)
    drain(sea_send.at[0], 2 * 16)
    sea_turned[...] = jnp.zeros_like(sea_turned)
    for h in range(2):
        lanes = slice(h * 128, (h + 1) * 128)
        rows = jnp.concatenate(
            [sea_raw[0, :, lanes], sea_raw[1, :, lanes], sea_raw[2, :, lanes], jnp.zeros((104, 128), jnp.float32)], axis=0)
        sea_turned[pl.ds(8 + h * 128, 128), :] = rows.T
    for q in range(12):
        column = q + 6
        here = sea_turned[pl.ds(pl.multiple_of(8 + r * WY, 8), ROW), :]
        sea_ext[pl.ds((q + 1) * ROW, ROW), :] = jnp.broadcast_to(here[:, column:column + 1], (ROW, 128))
        left = sea_turned[pl.ds(6 + r * WY, 2), :]
        sea_ext[pl.ds((q + 1) * ROW - 2, 2), :] = jnp.broadcast_to(left[:, column:column + 1], (2, 128))

    pltpu.make_async_copy(dk_raw, dk_raw, weights_sem.at[0]).wait()
    for u in range(LT):
        block = dk_raw[:, u * 128:(u + 1) * 128].T
        for i in range(8):
            k, t = divmod(8 * u + i, LT)
            wd[pl.ds(128 * t + SHARE * k, SHARE), :] = block[i * SHARE:(i + 1) * SHARE]

    def inside_pairs(step, begin, end):
        def one(n, c):
            advect_inside(step, 2 * n, 2)
            return c
        lax.fori_loop(begin, end, one, 0)

    def advect_pairs(step, begin, end):
        def one(n, c):
            take_rows(step, n, 2)
            advect(step, 2 * n, 2)
            return c
        lax.fori_loop(begin, end, one, 0)

    def advect_last(step):
        take_rows(step, PAIRS, 1)
        advect(step, LT - 1, 1)

    pltpu.make_async_copy(kl_raw, kl_raw, weights_sem.at[1]).wait()
    pltpu.make_async_copy(ks_raw, ks_raw, weights_sem.at[2]).wait()

    def enter_tile(t, c):
        prepare(t)
        turn(t)

        @pl.when(lax.rem(t, 2) == 1)
        def _():
            send_rows(0, t - 1, 2, rows_arrived(0, lax.div(t, 2)))

        @pl.when(t == 3)
        def _():
            send_sides(0, 0)

        @pl.when(t == 7)
        def _():
            send_sides(0, 1)

        return c

    total[...] = jnp.zeros_like(total)
    lax.fori_loop(0, LT, enter_tile, 0)
    send_sides(0, 2)
    send_rows(0, LT - 1, 1, rows_arrived(0, PAIRS))
    column_currents(0)
    take_columns(0, 0)
    inside_pairs(0, 0, 2)
    row_currents(0)
    take_corners(0, 0)
    advect_pairs(0, 0, 2)
    take_columns(0, 1)
    inside_pairs(0, 2, PAIRS)
    take_corners(0, 1)
    advect_pairs(0, 2, PAIRS)
    take_columns(0, 2)
    advect_inside(0, LT - 1, 1)
    take_corners(0, 2)
    advect_last(0)

    lane_row = lax.broadcasted_iota(jnp.int32, (WY, 128), 1)
    even = lax.rem(lane_row, 2) == 0
    sign = jnp.where(even, DT_OCEAN, -DT_OCEAN)

    def turn_back(t, value):
        for half in range(2):
            back[t, half] = value[half * 128:(half + 1) * 128].T
        for copy in exit_copies(t):
            copy.start()
        for half in range(2):
            got[t, r, half] = back[t, half, share_rows(r), :]

    def source(step, first_tile, count, last):
        lanes = pl.ds(pl.multiple_of(first_tile * 128, 128), count * 128)
        inter = jnp.dot(rounded[...], wl[:, lanes], preferred_element_type=jnp.float32)
        inter += jnp.dot(squared[...], ws[:, lanes], preferred_element_type=jnp.float32)
        fresh = []
        for k in range(count):
            old = e2[first_tile + k]
            new = old + inter[:, k * 128:(k + 1) * 128] * old * weight[...]
            if last:
                turn_back(first_tile + k, new)
            else:
                for x in range(WX):
                    ext[step + 1, first_tile + k, pl.ds((FIRST + x) * ROW, WY), :] = new[x * WY:(x + 1) * WY]
            fresh.append(new.astype(jnp.bfloat16))
        fresh = jnp.concatenate(fresh, axis=1) if count > 1 else fresh[0]
        drift[...] += jnp.dot(fresh, wd[lanes, :], preferred_element_type=jnp.float32)

    def swim(step, last):
        def one(x, c):
            at = own_row(x)
            old = ext[step, OT, pl.ds(at, WY), :]
            lap = (ext[step, OT, pl.ds(at + ROW, WY), :] + ext[step, OT, pl.ds(at - ROW, WY), :]
                   + (ext[step, OT, pl.ds(at + 1, WY), :] + ext[step, OT, pl.ds(at - 1, WY), :]) - 4.0 * old)
            here = pl.ds(pl.multiple_of(x * WY, WY), WY)
            pushed = old + drift[here, :]
            other = jnp.where(even, pltpu.roll(pushed, 127, 1), pltpu.roll(pushed, 1, 1))
            new = (old + (sign * other + DT_OCEAN * lap)) * sea_ext[pl.ds(at, WY), :]
            if last:
                drift[here, :] = new
            else:
                ext[step + 1, OT, pl.ds(at, WY), :] = new
            return c
        lax.fori_loop(0, WX, one, 0)
        if last:
            turn_back(OT, drift[...])

    def react(step, last):
        weigh()
        drift[...] = jnp.zeros_like(drift)

        def source_pair(n, c):
            source(step, 2 * n, 2, last)
            if not last:
                @pl.when(n < 2)
                def _():
                    send_rows(step + 1, 2 * n, 2, rows_arrived(step + 1, n))

                @pl.when(n == 1)
                def _():
                    send_sides(step + 1, 0)
            return c

        lax.fori_loop(0, LT // 2, source_pair, 0)
        source(step, LT - 1, 1, last)
        swim(step, last)

    def whole_step(step, c):
        react(step, False)
        send_ocean(step + 1)
        send_sides(step + 1, 1)
        send_sides(step + 1, 2)
        for n in range(2, PAIRS):
            send_rows(step + 1, 2 * n, 2, rows_arrived(step + 1, n))
        send_rows(step + 1, LT - 1, 1, rows_arrived(step + 1, PAIRS))
        later = step + 1
        own_currents(later)
        column_currents(later)
        total[...] = jnp.zeros_like(total)
        for group in range(OCEAN):
            take_columns(later, group)
        inside_pairs(later, 0, PAIRS)
        advect_inside(later, LT - 1, 1)
        row_currents(later)
        for group in range(OCEAN):
            take_corners(later, group)
        advect_pairs(later, 0, PAIRS)
        advect_last(later)
        return c

    lax.fori_loop(0, STEPS - 1, whole_step, 0)
    react(STEPS - 1, True)

    def leave(t, carry):
        drain(out_recv.at[t], (PARTS - 1) * 2 * SHARE)
        for octet in range(2):
            for h in range(2):
                for half in range(2):
                    blocks = swap_blocks([got[t, 4 * h + j, half, pl.ds(octet * 8, 8), :] for j in range(4)])
                    for i in range(4):
                        spec_out[h, pl.ds(t * 128 + octet * 64 + 4 * half + i, 8, stride=8), :] = blocks[i]
        for h in range(2):
            pltpu.make_async_copy(
                spec_out.at[h, tile_rows(t)], eo.at[tile_rows(t), half_lanes(h)], store.at[0]).start()
        return carry

    lax.fori_loop(0, LT, leave, 0)
    drain(out_recv.at[OT], (PARTS - 1) * 2 * SHARE)
    for comp in range(2):
        for h in range(2):
            for half in range(2):
                blocks = swap_blocks([got[OT, 4 * h + j, half, pl.ds(comp, 8, stride=2), :] for j in range(4)])
                for i in range(4):
                    swim_out[h, pl.ds(64 * comp + 4 * half + i, 8, stride=8), :] = blocks[i]
    for h in range(2):
        pltpu.make_async_copy(swim_out.at[h], oo.at[:, half_lanes(h)], store.at[0]).start()
    drain(store.at[0], 2 * NB + 256)
    drain(in_send.at[0], NT * (PARTS - 1) * 2 * SHARE)
    drain(out_send.at[0], NT * (PARTS - 1) * 2 * SHARE)
    for step in range(STEPS):
        drain(halo_send.at[step], NT * (4 * WY + 2 * SMALL) + len(SIDES) * 4 * 8)


def per_device(spectrum, sea_mask, kernel_linear, kernel_square, drift_kernel, ocean):
    y = spectrum.shape[2]
    any_ = pl.BlockSpec(memory_space=pl.ANY)
    vmem = pl.BlockSpec(memory_space=pltpu.VMEM)
    f32, bf16 = jnp.float32, jnp.bfloat16
    dma = pltpu.SemaphoreType.DMA
    eo, oo = pl.pallas_call(
        kernel,
        out_shape=(jax.ShapeDtypeStruct((NB, y), f32), jax.ShapeDtypeStruct((128, y), f32)),
        in_specs=[any_, any_, vmem, any_, any_, any_, vmem],
        out_specs=(any_, any_),
        scratch_shapes=[
            pltpu.VMEM((2, NB, 128), f32),
            pltpu.VMEM((2, 128, 128), f32),
            pltpu.VMEM((NT, PARTS, 2, SHARE, 128), f32),
            pltpu.VMEM((NT, 2, 128, 128), f32),
            pltpu.VMEM((STEPS, NT, EXT, 128), f32),
            pltpu.VMEM((3, 8, y), f32),
            pltpu.VMEM((8 + 256 + ROW, 128), f32),
            pltpu.VMEM((EXT, 128), f32),
            pltpu.VMEM((LT * EXT, 128), f32),
            pltpu.VMEM((LT, COLS, 128), f32),
            pltpu.VMEM((COLS, NB), bf16),
            pltpu.VMEM((COLS, NB), bf16),
            pltpu.VMEM((EXT, 128), f32),
            pltpu.VMEM((EXT, 128), f32),
            pltpu.VMEM((COLS, 128), f32),
            pltpu.VMEM((COLS, 128), f32),
            pltpu.VMEM((COLS, 128), f32),
            pltpu.VMEM((LT, PARTS, SHARE, NB), bf16),
            pltpu.VMEM((LT, PARTS, SHARE, NB), bf16),
            pltpu.VMEM((128, NB), bf16),
            pltpu.VMEM((NB, NB), bf16),
            pltpu.VMEM((NB, NB), bf16),
            pltpu.VMEM((NB, 128), bf16),
            pltpu.VMEM((STEPS, 2, NT, 2, WX, 128), f32),
            pltpu.VMEM((STEPS, 2, NT, 2, WX, 128), f32),
            pltpu.VMEM((STEPS, len(SIDES), 4, 8, 128), f32),
            pltpu.VMEM((STEPS, len(SIDES), 4, 8, 128), f32),
            pltpu.VMEM((NT, 2, 128, 128), f32),
            pltpu.VMEM((NT, PARTS, 2, SHARE, 128), f32),
            pltpu.VMEM((2, NB, 128), f32),
            pltpu.VMEM((2, 128, 128), f32),
            dma((1,)),
            dma((NT,)),
            dma((STEPS,)),
            dma((STEPS, PAIRS + 1 + 2 * len(SIDES))),
            dma((1,)),
            dma((1,)),
            dma((1,)),
            dma((NT,)),
            dma((NT,)),
            dma((3,)),
            dma((1,)),
        ],
        compiler_params=pltpu.CompilerParams(
            collective_id=0, has_side_effects=True, vmem_limit_bytes=60 * 1024 * 1024
        ),
        name="coupled",
    )(
        spectrum.reshape(NB, y),
        ocean.reshape(128, y),
        sea_mask,
        kernel_linear.reshape(PARTS, LT, SHARE, NB),
        kernel_square.reshape(PARTS, LT, SHARE, NB),
        drift_kernel,
        jnp.asarray(group_speeds()),
    )
    return eo.reshape(spectrum.shape), oo.reshape(ocean.shape)


def solution(mesh):
    return jax.shard_map(
        per_device,
        mesh=mesh,
        in_specs=(
            P("bins", "geo", None),
            P("geo", None),
            P(),
            P(),
            P(),
            P(None, "bins", "geo", None),
        ),
        out_specs=(P("bins", "geo", None), P(None, "bins", "geo", None)),
        check_vma=False,
    )
```
